768 devices in a mesh: kpt: 4 (over x), band: 16 (over y, core), plane: 12 (over z).
Axes of the slice: x: 4, y: 8, z: 12, core: 2. Of those that a mesh axis runs over, the one named last changes fastest.
Arguments:
- wavefunctions: float32 [4, 16, 2, 1920, 96], P('kpt', 'band', None, 'plane'), may hold values from -6 to 6
- resident: float32 [4, 256, 2, 1920, 96], P('kpt', 'band', None, 'plane'), may hold values from -0.078125 to 0.078125
- potential: float32 [96, 9216], P('plane'), may hold values from -5 to 5
- stick_column_table: int32 [4, 1920], P('kpt'), may hold values from 0 to 9216, as said below
- kpoint: float32 [4, 3], P('kpt'), may hold values from -0.5 to 0.5
Outputs:
- residual: float32 [4, 16, 2, 1920, 96], P('kpt', 'band', None, 'plane')
The draws below stay inside these ranges and needn't reach their ends.
Inputs may be any that keep to these rules, and one draw needn't show every extreme that they name: `stick_column_table`: each row lists every column ix * 96 + iy whose signed frequencies satisfy mx^2 + my^2 <= 24^2 exactly once and no other column; every other slot holds 9216 and is empty. Slots p * 160 to (p + 1) * 160 - 1 are those of plane index p, and in every row the slots of some plane index are all live.
All inputs are finite; a program needn't handle non-finite values.
Results may differ from the reference program's by a relative error of at most 0.0003.
Values sent between devices are 32-bit elements; how exact they have to be, the bound alone decides.
A program may use at most 64 MiB of HBM per device.

```python
import jax
import jax.numpy as jnp
from jax import lax

NG = 96
STICKS = 1920
RES = 256
KPOINT_TOTAL = 4
BANDS = 16
STK_DEV = 160


def stick_row(row_key):
    first_key, second_key, third_key = jax.random.split(row_key, 3)
    column_list = jnp.arange(NG * NG, dtype=jnp.int32)
    column_x = column_list // NG
    column_y = column_list % NG
    signed_x = jnp.where(column_x < NG // 2, column_x, column_x - NG)
    signed_y = jnp.where(column_y < NG // 2, column_y, column_y - NG)
    radius = NG // 4
    inside = signed_x * signed_x + signed_y * signed_y <= radius * radius
    column_rank = jax.random.permutation(first_key, NG * NG).astype(jnp.int32)
    column_score = jnp.where(inside, column_rank, column_rank + NG * NG)
    column_order = jnp.argsort(column_score, stable=True).astype(jnp.int32)
    count = jnp.sum(inside.astype(jnp.int32))
    slots = jnp.arange(STICKS, dtype=jnp.int32)
    chosen = jnp.where(slots < count, column_order[:STICKS], NG * NG)
    full_owner = jax.random.randint(second_key, (), 0, STICKS // STK_DEV)
    slot_rank = jax.random.permutation(third_key, STICKS).astype(jnp.int32)
    slot_score = jnp.where(slots // STK_DEV == full_owner, slot_rank - STICKS, slot_rank)
    slot_order = jnp.argsort(slot_score, stable=True).astype(jnp.int32)
    return jnp.zeros((STICKS,), jnp.int32).at[slot_order].set(chosen)


def draw_stick_column_table(key, part):
    row_keys = jax.random.split(jax.random.fold_in(key, 17), KPOINT_TOTAL)
    return jax.vmap(stick_row)(row_keys)


def level_of(key, extent, shards, low, top_value):
    def one(axis_at, shards_of):
        heights = jax.random.uniform(jax.random.fold_in(jax.random.fold_in(key, 6), axis_at), (shards_of,), jnp.float32, low / len(shards), top_value / len(shards))
        return jnp.repeat(jnp.exp(heights), extent[axis_at] // shards_of).reshape((-1,) + (1,) * (len(extent) - axis_at - 1))

    loudness = one(*shards[0])
    for cut in shards[1:]:
        loudness = loudness * one(*cut)
    return loudness


def bell_draw(stream_key, shape, scale, most, shards=(), kind=jnp.bfloat16):
    array = jax.random.normal(stream_key, shape, jnp.float32) * scale
    if len(shards) > 0:
        array = level_of(stream_key, shape, shards, -0.22, 0.18) * array
    return jnp.clip(array, min=-most, max=most).astype(kind)


def setup_inputs(seed: int = 0) -> dict:
    splits = jax.random.split(jax.random.key(seed), 6)
    return {
        "wavefunctions": bell_draw(splits[0], (KPOINT_TOTAL, BANDS, 2, STICKS, NG), 1.0, 6.0, ((0, 4), (1, 16), (3, 12)), jnp.float32),
        "resident": bell_draw(splits[1], (KPOINT_TOTAL, RES, 2, STICKS, NG), (3 * NG * NG // 4) ** -0.5, 0.078125, ((0, 4), (1, 16), (3, 12)), jnp.float32),
        "potential": bell_draw(splits[2], (NG, NG * NG), 1.0, 5.0, ((0, 12),), jnp.float32),
        "stick_column_table": draw_stick_column_table(jax.random.fold_in(splits[5], 71), 0),
        "kpoint": jnp.clip(jax.random.uniform(splits[4], (KPOINT_TOTAL, 3), jnp.float32, -0.5, 0.5) * level_of(splits[4], (KPOINT_TOTAL, 3), ((0, 4),), -0.4, 0.0), -0.5, 0.5),
    }


KINETIC = 12.0
HIGHEST = lax.Precision.HIGHEST


def signed_index(values):
    return jnp.where(values < NG // 2, values, values - NG)


def images_one(plane_coefficients, column_list, kpoint_shift, potential):
    live = column_list < NG * NG
    safe_columns = jnp.where(live, column_list, 0)
    values = plane_coefficients[0] + 1j * plane_coefficients[1]
    spectrum = jnp.zeros((NG * NG, NG), values.dtype).at[column_list].set(values, mode="drop")
    field = jnp.fft.ifftn(spectrum.reshape(NG, NG, NG)) * (NG ** 3)
    weights = jnp.transpose(potential.reshape(NG, NG, NG), (1, 2, 0))
    returned = jnp.fft.fftn(field * weights) / (NG ** 3)
    picked = returned.reshape(NG * NG, NG)[safe_columns]
    freq_x = signed_index(safe_columns // NG).astype(jnp.float32) + kpoint_shift[0]
    freq_y = signed_index(safe_columns % NG).astype(jnp.float32) + kpoint_shift[1]
    freq_z = signed_index(jnp.arange(NG, dtype=jnp.int32)).astype(jnp.float32) + kpoint_shift[2]
    kinetic = (KINETIC / (NG * NG)) * ((freq_x * freq_x + freq_y * freq_y)[:, None] + (freq_z * freq_z)[None, :])
    active_float_mask = live.astype(jnp.float32)[:, None]
    image_real = (jnp.real(picked) + kinetic * plane_coefficients[0]) * active_float_mask
    image_imag = (jnp.imag(picked) + kinetic * plane_coefficients[1]) * active_float_mask
    return jnp.stack([image_real, image_imag])


def reference(wavefunctions, resident, potential, stick_column_table, kpoint):
    outputs = []
    for kpoint_index in range(KPOINT_TOTAL):
        column_list = stick_column_table[kpoint_index]
        active_float_mask = (column_list < NG * NG).astype(jnp.float32)
        plane_coefficients = wavefunctions[kpoint_index] * active_float_mask[None, None, :, None]
        kpoint_shift = kpoint[kpoint_index]
        images = lax.map(lambda single: images_one(single, column_list, kpoint_shift, potential), plane_coefficients)
        basis_vectors = resident[kpoint_index] * active_float_mask[None, None, :, None]
        basis_vectors_real = basis_vectors[:, 0].reshape(RES, STICKS * NG)
        basis_vectors_imag = basis_vectors[:, 1].reshape(RES, STICKS * NG)
        image_real = images[:, 0].reshape(BANDS, STICKS * NG)
        image_imag = images[:, 1].reshape(BANDS, STICKS * NG)
        margin_real = jnp.dot(basis_vectors_real, image_real.T, precision=HIGHEST) + jnp.dot(basis_vectors_imag, image_imag.T, precision=HIGHEST)
        margin_imag = jnp.dot(basis_vectors_real, image_imag.T, precision=HIGHEST) - jnp.dot(basis_vectors_imag, image_real.T, precision=HIGHEST)
        correction_real = jnp.dot(margin_real.T, basis_vectors_real, precision=HIGHEST) - jnp.dot(margin_imag.T, basis_vectors_imag, precision=HIGHEST)
        correction_imag = jnp.dot(margin_real.T, basis_vectors_imag, precision=HIGHEST) + jnp.dot(margin_imag.T, basis_vectors_real, precision=HIGHEST)
        residual = jnp.stack([image_real - correction_real, image_imag - correction_imag], axis=1)
        outputs.append(residual.reshape(BANDS, 2, STICKS, NG))
    return jnp.stack(outputs)
```

```python
import functools
import math

import jax
import jax.numpy as jnp
import numpy as np
from jax import lax
from jax.experimental import pallas as pl
from jax.experimental.pallas import tpu as pltpu
from jax.sharding import PartitionSpec as P

NG = 96
KINETIC = 12.0
HIGHEST = lax.Precision.HIGHEST
MESH = pl.DeviceIdType.MESH
RAD = NG // 4
IXP = 64
LP = 128
F32 = jnp.float32
BF16 = jnp.bfloat16


def split_np(table):
    table = np.asarray(table, np.float32)
    high = table.astype(jnp.bfloat16)
    low = (table - high.astype(np.float32)).astype(jnp.bfloat16)
    return high, low


def tables():
    turn = 2.0 * math.pi / NG
    grid = np.arange(NG)
    full = np.outer(grid, grid) % NG * turn
    tz = np.concatenate([np.cos(full), np.sin(full)], axis=0)
    signed = np.arange(IXP) - RAD
    inside = (np.arange(IXP) <= 2 * RAD).astype(np.float64)
    part = np.outer(grid, signed) % NG * turn
    cosine = np.cos(part) * inside
    sine = np.sin(part) * inside
    pad = np.zeros((LP - NG, IXP))
    cy = np.concatenate([cosine, pad])
    sy = np.concatenate([sine, pad])
    ty = np.concatenate([cy, sy, -sy, cy], axis=0)
    xf = np.block([[cosine, -sine], [sine, cosine]])
    xb = np.block([[cosine.T, sine.T], [-sine.T, cosine.T]]) / float(NG) ** 3
    zb = np.zeros((LP, 2 * LP))
    zb[:NG, :NG] = np.cos(full)
    zb[:NG, LP : LP + NG] = np.sin(full)
    return [part for table in (tz, ty, xf, xb, zb) for part in split_np(table)]


def split(value):
    high = value.astype(BF16)
    low = (value - high.astype(F32)).astype(BF16)
    return high, low


def dot3(left, right, axes):
    dims = (((axes[0],), (axes[1],)), ((), ()))

    def one(a, b):
        return lax.dot_general(a, b, dims, preferred_element_type=F32)

    return one(left[0], right[0]) + (one(left[1], right[0]) + one(left[0], right[1]))


def local_kernel(
    nz, slots, planes,
    wf_ref, table_ref, pot_ref, kp_ref,
    tzh, tzl, tyh, tyl, xfh, xfl, xbh, xbl, zbh, zbl,
    out_ref,
    send1, recv1, send2, recv2, bth, btl, lhh, lhl, mask, vall, pick, extra, trans, livecol,
    ssem1, rsem1, ssem2, rsem2,
    projector,
):
    me = lax.axis_index("plane")
    total = nz * slots
    barrier = pltpu.get_barrier_semaphore()
    for step in range(1, nz):
        pl.semaphore_signal(barrier, inc=1, device_id={"plane": lax.rem(me + step, nz)}, device_id_type=MESH)

    greeted = projector.greet(barrier)

    forward = (tzh[...], tzl[...])
    from_real = dot3(forward, split(wf_ref[0]), (1, 1))
    from_imag = dot3(forward, split(wf_ref[1]), (1, 1))
    real = from_real[:NG] - from_imag[NG:]
    imag = from_imag[:NG] + from_real[NG:]
    send1[:, :, 0:slots] = real.reshape(nz, planes, slots)
    send1[:, :, slots : 2 * slots] = imag.reshape(nz, planes, slots)
    send1[:, :, 2 * slots :] = jnp.zeros((nz, planes, send1.shape[2] - 2 * slots), F32)
    pl.semaphore_wait(barrier, nz - 1 + greeted)

    def exchange(source, target, ssem, rsem):
        copies = []
        for step in range(1, nz):
            there = lax.rem(me + step, nz)
            copies.append(
                pltpu.make_async_remote_copy(
                    src_ref=source.at[there],
                    dst_ref=target.at[me],
                    send_sem=ssem.at[step],
                    recv_sem=rsem.at[step],
                    device_id={"plane": there},
                    device_id_type=MESH,
                )
            )
        order = sorted(range(nz - 1), key=lambda i: -min(i + 1, nz - 1 - i))
        for i in order:
            copies[i].start()
        target[me] = source[me]
        return copies

    copies1 = exchange(send1, recv1, ssem1, rsem1)

    projector.start_resident()

    columns = table_ref[...].astype(F32)
    alive = columns < float(NG * NG)
    ix = ((columns + 0.5) * (1.0 / NG)).astype(jnp.int32).astype(F32)
    iy = columns - ix * NG
    mx = jnp.where(ix < NG // 2, ix, ix - NG)
    my = jnp.where(iy < NG // 2, iy, iy - NG)
    kx = jnp.where(alive, mx + RAD, -1.0)
    ky = jnp.where(alive, my + RAD, -1.0)
    rows = lax.broadcasted_iota(jnp.int32, (IXP, total), 0).astype(F32)
    hot_x = jnp.where(rows == kx, 1.0, 0.0)
    hot_y = jnp.where(rows == ky, 1.0, 0.0).astype(BF16)
    mask[:, 0:total] = hot_x
    mask[:, total:] = hot_x
    for c in range(2):
        for tab, into in ((tyh, bth), (tyl, btl)):
            into[:, c * total : (c + 1) * total] = jnp.dot(
                tab[c * 2 * LP : (c + 1) * 2 * LP, :], hot_y, preferred_element_type=F32
            ).astype(BF16)
    fx = mx + kp_ref[0, 0]
    fy = my + kp_ref[0, 1]
    sheet = fx * fx + fy * fy
    live = jnp.where(alive, 1.0, 0.0)
    for q in range(nz):
        extra[q, 0:1, 0:slots] = sheet[:, q * slots : (q + 1) * slots]
        extra[q, 1:2, 0:slots] = live[:, q * slots : (q + 1) * slots]

    for copy in copies1:
        copy.wait()
    for q in range(nz):
        vall[:, q * slots : (q + 1) * slots] = recv1[q, :, 0:slots]
        vall[:, total + q * slots : total + (q + 1) * slots] = recv1[q, :, slots : 2 * slots]

    wide = 256
    @pl.loop(0, 2 * total // wide)
    def _(chunk):
        lanes = pl.ds(pl.multiple_of(chunk * wide, wide), wide)
        hot = mask[:, lanes].astype(BF16)
        values = vall[:, lanes]
        for z in range(planes):
            row = jnp.broadcast_to(values[z : z + 1], (16, wide))
            high, low = split(row)
            for g in range(IXP // 16):
                part = hot[g * 16 : (g + 1) * 16]
                lhh[z * IXP + g * 16 : z * IXP + (g + 1) * 16, lanes] = part * high
                lhl[z * IXP + g * 16 : z * IXP + (g + 1) * 16, lanes] = part * low

    rows_done = dot3((lhh[...], lhl[...]), (bth[...], btl[...]), (1, 1))
    to_x = (xfh[...], xfl[...])
    to_k = (xbh[...], xbl[...])
    spectrum = []
    for z in range(0, planes, 2):
        a = rows_done[z * IXP : (z + 1) * IXP]
        b = rows_done[(z + 1) * IXP : (z + 2) * IXP]
        pair = jnp.concatenate(
            [jnp.concatenate([a[:, :LP], b[:, :LP]], 1), jnp.concatenate([a[:, LP:], b[:, LP:]], 1)], 0
        )
        field = dot3(to_x, split(pair), (1, 0))
        zeros = jnp.zeros((NG, LP - NG), F32)
        weight = jnp.concatenate([pot_ref[z], zeros, pot_ref[z + 1], zeros], 1)
        product = field * jnp.concatenate([weight, weight], 0)
        back = dot3(to_k, split(product), (1, 0))
        for h in range(2):
            spectrum.append(
                jnp.concatenate(
                    [back[:IXP, h * LP : (h + 1) * LP], back[IXP:, h * LP : (h + 1) * LP]], 1
                )
            )
    spread = split(jnp.concatenate(spectrum, 0))

    for chunk in range(2 * total // wide):
        lanes = slice(chunk * wide, (chunk + 1) * wide)
        found = dot3(spread, (bth[:, lanes], btl[:, lanes]), (1, 0))
        found = found.reshape(planes, IXP, wide) * mask[:, lanes][None]
        pick[:, lanes] = jnp.sum(found, axis=1)

    send2[:, :, 2 * slots :] = jnp.zeros((nz, planes, send2.shape[2] - 2 * slots), F32)
    for q in range(nz):
        send2[q, :, 0:slots] = pick[:, q * slots : (q + 1) * slots]
        send2[q, :, slots : 2 * slots] = pick[:, total + q * slots : total + (q + 1) * slots]
    copies2 = exchange(send2, recv2, ssem2, rsem2)
    trans[NG:, :] = jnp.zeros((LP - NG, trans.shape[1]), F32)
    trans[NG : NG + 2, 0:slots] = extra[me, 0:2, 0:slots]
    freq = lax.broadcasted_iota(jnp.int32, (1, NG), 1)
    fz = jnp.where(freq < NG // 2, freq, freq - NG).astype(F32) + kp_ref[0, 2]
    projector.finish_resident()
    projector.flatten_resident()
    for copy in copies2:
        copy.wait()
    trans[0:NG, :] = recv2[...].reshape(NG, trans.shape[1])
    turned = trans[...].T
    both = turned[: 2 * slots]
    result = dot3(split(both), (zbh[...], zbl[...]), (1, 0))
    alive = turned[:slots, NG + 1 : NG + 2]
    kinetic = (KINETIC / (NG * NG)) * (turned[:slots, NG : NG + 1] + fz * fz) * alive
    images = (
        (result[:slots, :LP] + result[slots:, LP:])[:, :NG] + kinetic * wf_ref[0],
        (result[slots:, :LP] - result[:slots, LP:])[:, :NG] + kinetic * wf_ref[1],
    )
    projector.pack(images)
    for c in range(2):
        out_ref[c] = images[c]
    livecol[...] = jnp.broadcast_to(alive, livecol.shape)
    projector.gather()
    margin = projector.margin()
    projector.correct(margin)
    projector.scatter()
    for c in range(2):
        out_ref[c] = out_ref[c] - livecol[...] * projector.correction(c)


ORDER = (0, 1, 7, 2, 6, 3, 5, 4)


class Projector:
    def __init__(self, nz, slots, rows, refs):
        (self.res, self.dbuf, self.dh, self.dl, self.packed, self.abuf, self.ih, self.il, self.mpair, self.mall,
         self.cbuf, self.rbuf, self.fbuf, self.unpacked,
         self.dsem, self.psem, self.agsem, self.mpsem, self.mssem, self.mrsem, self.rssem, self.fsem) = refs
        self.nz, self.half, self.rows = nz, slots // 2, rows
        self.lines = self.half * NG // LP
        self.block = 2 * self.lines
        band = lax.axis_index("band")
        nb = 16
        self.me = lax.axis_index("plane")
        self.core = lax.rem(band, 2)
        self.partner = {"band": band + 1 - 2 * self.core}
        self.right = {"band": lax.rem(band + 2, nb)}
        self.left = {"band": lax.rem(band + nb - 2, nb)}

    def remote(self, src, dst, send, recv, device):
        return pltpu.make_async_remote_copy(
            src_ref=src, dst_ref=dst, send_sem=send, recv_sem=recv, device_id=device, device_id_type=MESH
        )

    def greet(self, barrier):
        for device in (self.partner, self.right, self.left):
            pl.semaphore_signal(barrier, inc=1, device_id=device, device_id_type=MESH)
        return 3

    def slab(self, i):
        place = (self.core * self.rows * 2 + i) * self.half
        return self.dbuf.at[pl.ds(pl.multiple_of(place, 8), self.half), :]

    def local_fetch(self, i):
        own = pl.ds(pl.multiple_of(self.core * self.half, 8), self.half)
        return pltpu.make_async_copy(self.res.at[i, own, :], self.slab(i), self.dsem.at[0, i])

    def swap_resident(self, i):
        other = pl.ds(pl.multiple_of((1 - self.core) * self.half, 8), self.half)
        return self.remote(
            self.res.at[i, other, :], self.slab(i), self.dsem.at[1, i], self.dsem.at[2, i], self.partner
        )

    def start_resident(self):
        @pl.loop(0, 2 * self.rows)
        def _(i):
            self.swap_resident(i).start()
            self.local_fetch(i).start()

    def finish_resident(self):
        @pl.loop(0, 2 * self.rows)
        def _(i):
            self.swap_resident(i).wait()
            self.local_fetch(i).wait()

    def flatten_resident(self):
        third = self.lines // 3
        span = 2 * self.half

        @pl.loop(0, third)
        def _(i):
            for c in range(2):
                for group in range(2 * self.rows // 16):
                    base = group * 16 * span + c * self.half + i
                    tail = self.dbuf[pl.ds(base + self.lines, 16, stride=span), :]
                    for k in range(3):
                        head = self.dbuf[pl.ds(base + k * third, 16, stride=span), :]
                        line = jnp.concatenate([head, tail[:, k * 32 : (k + 1) * 32]], 1)
                        lanes = pl.ds(pl.multiple_of((k * third + i) * LP, LP), LP)
                        at = slice(c * 2 * self.rows + group * 16, c * 2 * self.rows + group * 16 + 16)
                        self.dh[at, lanes], self.dl[at, lanes] = split(line)

    def at(self, rel, sub):
        place = ORDER.index(rel % 8) * 2 + sub
        return pl.ds(pl.multiple_of(place * self.block, 8), self.block)

    def pack(self, images):
        third = self.lines // 3
        for hh in range(2):
            for c in range(2):
                part = images[c][hh * self.half : (hh + 1) * self.half]
                self.packed[hh, c * self.lines : (c + 1) * self.lines, 0:NG] = part[: self.lines, :NG]
                for k in range(3):
                    start = c * self.lines + k * third
                    self.packed[hh, start : start + third, NG:LP] = part[self.lines :, k * 32 : (k + 1) * 32]

    def gather(self):
        mine, other = self.core, 1 - self.core
        pair = self.remote(
            self.packed.at[other], self.abuf.at[self.at(0, mine)], self.psem.at[0], self.psem.at[1], self.partner
        )
        pair.start()
        self.abuf[self.at(0, mine), :] = self.packed[mine]

        def hop(way, step, sub):
            sign = -1 if way == 0 else 1
            return self.remote(
                self.abuf.at[self.at(sign * step, sub)],
                self.abuf.at[self.at(sign * (step + 1), sub)],
                self.agsem.at[0, way, step, sub],
                self.agsem.at[1, way, step, sub],
                self.right if way == 0 else self.left,
            )

        started = []
        for step in range(4):
            for turn, sub in enumerate((mine, other)):
                if step == 0 and turn == 1:
                    pair.wait()
                for way in range(2):
                    if step == 3:
                        if turn == 1:
                            continue
                        sub = way
                    if step > 0:
                        hop(way, step - 1, sub).wait_recv()
                    copy = hop(way, step, sub)
                    copy.start()
                    started.append(copy)
                    if step == 3:
                        hop(way, 2, 1 - way).wait_recv()
        self.started = started
        self.hop = hop

    def flatten_images(self):
        @pl.loop(0, self.lines)
        def _(r):
            lanes = pl.ds(pl.multiple_of(r * LP, LP), LP)
            for c in range(2):
                value = self.abuf[pl.ds(c * self.lines + r, 16, stride=self.block), :]
                self.ih[c * 16 : (c + 1) * 16, lanes], self.il[c * 16 : (c + 1) * 16, lanes] = split(value)

    def margin(self):
        for way in range(2):
            self.hop(way, 3, way).wait_recv()
        for copy in self.started:
            copy.wait_send()
        self.flatten_images()
        count = 2 * self.rows
        gram = dot3((self.ih[...], self.il[...]), (self.dh[...], self.dl[...]), (1, 1))
        real = gram[:16, :count] + gram[16:, count:]
        imag = gram[16:, :count] - gram[:16, count:]
        both = jnp.concatenate([real, imag], 1)
        self.mpair[0] = jnp.concatenate([both[:8], both[8:]], 1)
        swap = self.remote(self.mpair.at[0], self.mpair.at[1], self.mpsem.at[0], self.mpsem.at[1], self.partner)
        swap.start()
        swap.wait()
        self.mall[self.me] = self.mpair[0] + self.mpair[1]
        copies = []
        order = sorted(range(1, self.nz), key=lambda i: -min(i, self.nz - i))
        for step in order:
            there = lax.rem(self.me + step, self.nz)
            copy = self.remote(
                self.mall.at[self.me], self.mall.at[self.me],
                self.mssem.at[step], self.mrsem.at[step], {"plane": there},
            )
            copy.start()
            copies.append(copy)
        for copy in copies:
            copy.wait()
        flat = jnp.sum(self.mall[...], axis=0)
        both = jnp.concatenate([flat[:, : 2 * count], flat[:, 2 * count :]], 0)
        real, imag = both[:, :count], both[:, count:]
        return jnp.concatenate(
            [jnp.concatenate([real, -imag], 1), jnp.concatenate([imag, real], 1)], 0
        )

    def correct(self, margin):
        left = split(margin)
        batch = 4

        @pl.loop(0, self.lines // batch)
        def _(g):
            lanes = pl.ds(pl.multiple_of(g * batch * LP, LP), batch * LP)
            value = dot3(left, (self.dh[:, lanes], self.dl[:, lanes]), (1, 0))
            for i in range(batch):
                for c in range(2):
                    self.cbuf[pl.ds(c * self.lines + g * batch + i, 16, stride=self.block), :] = value[
                        c * 16 : (c + 1) * 16, i * LP : (i + 1) * LP
                    ]

    def scatter(self):
        def slot(way, k, sub):
            place = (way * 4 + k) * 2 + sub
            return pl.ds(place * self.block, self.block)

        def own(way, k, sub):
            return self.at(k if way == 0 else -k, sub)

        def hop(way, k, sub, source):
            return self.remote(
                source, self.rbuf.at[slot(way, k - 1, sub)],
                self.rssem.at[0, way, k - 1, sub], self.rssem.at[1, way, k - 1, sub],
                self.right if way == 0 else self.left,
            )

        sent = []
        for k in (4, 3, 2, 1, 0):
            for sub in range(2):
                for way in range(2):
                    first = 4 if sub == way else 3
                    if k > first:
                        continue
                    if k == first:
                        copy = hop(way, k, sub, self.cbuf.at[own(way, k, sub)])
                    else:
                        hop(way, k + 1, sub, self.cbuf.at[own(way, k + 1, sub)]).wait_recv()
                        if k == 0:
                            continue
                        here = slot(way, k, sub)
                        self.rbuf[here, :] = self.rbuf[here, :] + self.cbuf[own(way, k, sub), :]
                        copy = hop(way, k, sub, self.rbuf.at[here])
                    copy.start()
                    sent.append(copy)
        for sub in range(2):
            total = self.cbuf[self.at(0, sub), :] + self.rbuf[slot(0, 0, sub), :] + self.rbuf[slot(1, 0, sub), :]
            self.fbuf[sub] = total
        final = self.remote(
            self.fbuf.at[1 - self.core], self.fbuf.at[2], self.fsem.at[0], self.fsem.at[1], self.partner
        )
        final.start()
        for copy in sent:
            copy.wait_send()
        self.unpack(self.core, self.core)
        final.wait()
        self.unpack(2, 1 - self.core)

    def unpack(self, source, hh):
        third = self.lines // 3
        for c in range(2):
            start = c * self.lines
            self.unpacked[hh, c, 0 : self.lines, :] = self.fbuf[source, start : start + self.lines, 0:NG]
            for k in range(3):
                self.unpacked[hh, c, self.lines : self.half, k * 32 : (k + 1) * 32] = self.fbuf[
                    source, start + k * third : start + (k + 1) * third, NG:LP
                ]

    def correction(self, c):
        return jnp.concatenate([self.unpacked[0, c], self.unpacked[1, c]], 0)

    @staticmethod
    def scratch(nz, slots, rows):
        half = slots // 2
        lines = half * NG // LP
        block = 2 * lines
        dma = pltpu.SemaphoreType.DMA
        return [
            pltpu.VMEM((4 * rows * half, NG), F32),
            pltpu.VMEM((4 * rows, lines * LP), BF16),
            pltpu.VMEM((4 * rows, lines * LP), BF16),
            pltpu.VMEM((2, block, LP), F32),
            pltpu.VMEM((16 * block, LP), F32),
            pltpu.VMEM((32, lines * LP), BF16),
            pltpu.VMEM((32, lines * LP), BF16),
            pltpu.VMEM((2, 8, LP), F32),
            pltpu.VMEM((nz, 8, LP), F32),
            pltpu.VMEM((16 * block, LP), F32),
            pltpu.VMEM((16 * block, LP), F32),
            pltpu.VMEM((3, block, LP), F32),
            pltpu.VMEM((2, 2, half, NG), F32),
            dma((3, 2 * rows)), dma((2,)), dma((2, 2, 4, 2)), dma((2,)), dma((nz,)), dma((nz,)), dma((2, 2, 4, 2)), dma((2,)),
        ]


def kernel(nz, slots, planes, rows, *refs):
    inputs, rest = refs[:14], refs[14:]
    resident, out_ref = rest[0], rest[1]
    count = 18
    local_scratch, project_scratch = rest[2 : 2 + count], rest[2 + count :]
    projector = Projector(nz, slots, rows, (resident,) + project_scratch)
    local_kernel(nz, slots, planes, *inputs, out_ref, *local_scratch, projector=projector)


def on_device(wavefunctions, resident, potential, stick_column_table, kpoint, nz):
    slots = wavefunctions.shape[3]
    planes = potential.shape[0]
    rows = resident.shape[1]
    total = nz * slots
    lanes = -(-2 * slots // LP) * LP
    vmem = pl.BlockSpec(memory_space=pltpu.VMEM)
    consts = [jnp.asarray(t) for t in tables()]
    block = pltpu.VMEM((nz, planes, lanes), F32)
    dma = pltpu.SemaphoreType.DMA
    out = pl.pallas_call(
        functools.partial(kernel, nz, slots, planes, rows),
        out_shape=jax.ShapeDtypeStruct((2, slots, NG), F32),
        in_specs=[vmem, vmem, vmem, pl.BlockSpec(memory_space=pltpu.SMEM)]
        + [vmem] * len(consts)
        + [pl.BlockSpec(memory_space=pl.ANY)],
        out_specs=vmem,
        scratch_shapes=[
            block, block, block, block,
            pltpu.VMEM((2 * LP, 2 * total), BF16),
            pltpu.VMEM((2 * LP, 2 * total), BF16),
            pltpu.VMEM((planes * IXP, 2 * total), BF16),
            pltpu.VMEM((planes * IXP, 2 * total), BF16),
            pltpu.VMEM((IXP, 2 * total), F32),
            pltpu.VMEM((planes, 2 * total), F32),
            pltpu.VMEM((planes, 2 * total), F32),
            pltpu.VMEM((nz, 8, lanes), F32),
            pltpu.VMEM((LP, lanes), F32),
            pltpu.VMEM((slots, NG), F32),
            dma((nz,)), dma((nz,)), dma((nz,)), dma((nz,)),
        ]
        + Projector.scratch(nz, slots, rows),
        compiler_params=pltpu.CompilerParams(collective_id=0, has_side_effects=True),
    )(
        wavefunctions[0, 0], stick_column_table, potential.reshape(planes, NG, NG), kpoint, *consts,
        resident[0].reshape(2 * rows, slots, NG),
    )
    return out[None, None]


def solution(mesh):
    in_specs = (
        P("kpt", "band", None, "plane", None),
        P("kpt", "band", None, "plane", None),
        P("plane", None),
        P("kpt", None),
        P("kpt", None),
    )
    out_specs = P("kpt", "band", None, "plane", None)
    return jax.shard_map(
        functools.partial(on_device, nz=mesh.shape["plane"]),
        mesh=mesh, in_specs=in_specs, out_specs=out_specs, check_vma=False,
    )
```

```python
import functools
import math

import jax
import jax.numpy as jnp
import numpy as np
from jax import lax
from jax.experimental import pallas as pl
from jax.experimental.pallas import tpu as pltpu
from jax.sharding import PartitionSpec as P

NG = 96
KINETIC = 12.0
HIGHEST = lax.Precision.HIGHEST
MESH = pl.DeviceIdType.MESH
RAD = NG // 4
IXP = 64
LP = 128
F32 = jnp.float32
BF16 = jnp.bfloat16


def split_np(table):
    table = np.asarray(table, np.float32)
    high = table.astype(jnp.bfloat16)
    low = (table - high.astype(np.float32)).astype(jnp.bfloat16)
    return high, low


def tables():
    turn = 2.0 * math.pi / NG
    grid = np.arange(NG)
    full = np.outer(grid, grid) % NG * turn
    tz = np.concatenate([np.cos(full), np.sin(full)], axis=0)
    signed = np.arange(IXP) - RAD
    inside = (np.arange(IXP) <= 2 * RAD).astype(np.float64)
    part = np.outer(grid, signed) % NG * turn
    cosine = np.cos(part) * inside
    sine = np.sin(part) * inside
    pad = np.zeros((LP - NG, IXP))
    cy = np.concatenate([cosine, pad])
    sy = np.concatenate([sine, pad])
    ty = np.block([[cy, -sy], [sy, cy]])
    xf = np.block([[cosine, -sine], [sine, cosine]])
    xb = np.block([[cosine.T, sine.T], [-sine.T, cosine.T]]) / float(NG) ** 3
    zb = np.zeros((LP, 2 * LP))
    zb[:NG, :NG] = np.cos(full)
    zb[:NG, LP : LP + NG] = np.sin(full)
    return [np.stack(split_np(table)) for table in (tz, ty, xf, xb, zb)]


def split(value):
    high = value.astype(BF16)
    low = (value - high.astype(F32)).astype(BF16)
    return high, low


def dot3(left, right, axes):
    dims = (((axes[0],), (axes[1],)), ((), ()))

    def one(a, b):
        return lax.dot_general(a, b, dims, preferred_element_type=F32)

    return one(left[0], right[0]) + (one(left[1], right[0]) + one(left[0], right[1]))


def local_kernel(
    nz, slots, planes,
    inputs, out_ref,
    wf_ref, table_ref, pot_ref, kp_ref, tz, ty, xf, xb, zb, insem,
    send1, recv1, send2, recv2, bth, btl, lhh, lhl, mask, acc, sph, spl, tabx, weights, trans, livecol,
    ssem1, rsem1, ssem2, rsem2,
    projector,
):
    me = lax.axis_index("plane")
    lanes = send1.shape[2]
    barrier = pltpu.get_barrier_semaphore()
    for step in range(1, nz):
        pl.semaphore_signal(barrier, inc=1, device_id={"plane": lax.rem(me + step, nz)}, device_id_type=MESH)
    greeted = projector.greet(barrier)
    held = (wf_ref, table_ref, pot_ref, kp_ref, tz, ty, xf, xb, zb)
    fetches = [pltpu.make_async_copy(a, b, insem.at[i]) for i, (a, b) in enumerate(zip(inputs, held))]
    for i in (0, 4, 1, 5, 2, 3, 6, 7, 8):
        fetches[i].start()
    fetches[0].wait()
    fetches[4].wait()

    forward = (tz[0], tz[1])
    from_real = dot3(forward, split(wf_ref[0]), (1, 1))
    from_imag = dot3(forward, split(wf_ref[1]), (1, 1))
    real = from_real[:NG] - from_imag[NG:]
    imag = from_imag[:NG] + from_real[NG:]
    send1[:, :, 0:slots] = real.reshape(nz, planes, slots)
    send1[:, :, slots : 2 * slots] = imag.reshape(nz, planes, slots)
    send1[:, :, 2 * slots :] = jnp.zeros((nz, planes, lanes - 2 * slots), F32)
    pl.semaphore_wait(barrier, nz - 1 + greeted)

    def transfer(source, target, ssem, rsem, step):
        there = lax.rem(me + step, nz)
        return pltpu.make_async_remote_copy(
            src_ref=source.at[there],
            dst_ref=target.at[me],
            send_sem=ssem.at[step],
            recv_sem=rsem.at[step],
            device_id={"plane": there},
            device_id_type=MESH,
        )

    out1 = [transfer(send1, recv1, ssem1, rsem1, step) for step in range(1, nz)]
    for step in sorted(range(1, nz), key=lambda i: -min(i, nz - i)):
        out1[step - 1].start()
    projector.start_resident()
    for i in (1, 5, 2, 3, 6, 7, 8):
        fetches[i].wait()

    tabx[...] = jnp.full(tabx.shape, float(NG * NG), F32)
    columns = table_ref[...].astype(F32)
    for q in range(nz):
        part = columns[:, q * slots : (q + 1) * slots]
        tabx[q : q + 1, 0:slots] = part
        tabx[q : q + 1, slots : 2 * slots] = part

    def decode(column):
        ix = ((column + 0.5) * (1.0 / NG)).astype(jnp.int32).astype(F32)
        iy = column - ix * NG
        return jnp.where(ix < NG // 2, ix, ix - NG), jnp.where(iy < NG // 2, iy, iy - NG)

    def block_lanes(q):
        return pl.ds(pl.multiple_of(q * lanes, LP), lanes)

    second = lax.broadcasted_iota(jnp.int32, (1, lanes), 1) >= slots
    rows = lax.broadcasted_iota(jnp.int32, (2 * IXP, lanes), 0).astype(F32)

    @pl.loop(0, nz)
    def _(q):
        column = tabx[pl.ds(q, 1), :]
        alive = column < float(NG * NG)
        mx, my = decode(column)
        kx = jnp.where(alive, mx + RAD, -1.0)
        ky = jnp.where(alive, my + RAD + jnp.where(second, float(IXP), 0.0), -1.0)
        mask[:, block_lanes(q)] = jnp.where(rows[:IXP] == kx, 1.0, 0.0)
        hot = jnp.where(rows == ky, 1.0, 0.0).astype(BF16)
        for i, into in ((0, bth), (1, btl)):
            into[:, block_lanes(q)] = jnp.dot(ty[i], hot, preferred_element_type=F32).astype(BF16)

    zeros = jnp.zeros((weights.shape[0], LP - NG), F32)
    weights[:, NG:LP] = zeros
    for x in range(NG):
        weights[pl.ds(x, planes, stride=NG), 0:NG] = pot_ref[:, x * NG : (x + 1) * NG]

    for pair in range(nz // 2):
        offsets = ((nz - pair) % nz, pair + 1)
        owners = [lax.rem(me + offset, nz) for offset in offsets]
        side = pair % 2
        for place, (offset, q) in enumerate(zip(offsets, owners)):
            if offset == 0:
                values = send1[me]
            else:
                out1[(nz - offset) - 1].wait_recv()
                values = recv1[q]
            hot = mask[:, block_lanes(q)].astype(BF16)
            into = slice(place * lanes, (place + 1) * lanes)
            for z in range(planes):
                high, low = split(jnp.broadcast_to(values[z : z + 1], (16, lanes)))
                for g in range(IXP // 16):
                    part = hot[g * 16 : (g + 1) * 16]
                    at = slice(z * IXP + g * 16, z * IXP + (g + 1) * 16)
                    lhh[side, at, into] = part * high
                    lhl[side, at, into] = part * low
        phase = tuple(jnp.concatenate([b[:, block_lanes(q)] for q in owners], 1) for b in (bth, btl))
        term = dot3((lhh[side], lhl[side]), phase, (1, 1))
        acc[...] = term if pair == 0 else acc[...] + term

    to_x = (xf[0], xf[1])
    to_k = (xb[0], xb[1])
    for z in range(0, planes, 2):
        a = acc[z * IXP : (z + 1) * IXP]
        b = acc[(z + 1) * IXP : (z + 2) * IXP]
        joined = jnp.concatenate(
            [jnp.concatenate([a[:, :LP], b[:, :LP]], 1), jnp.concatenate([a[:, LP:], b[:, LP:]], 1)], 0
        )
        field = dot3(to_x, split(joined), (1, 0))
        weight = jnp.concatenate([weights[z * NG : (z + 1) * NG], weights[(z + 1) * NG : (z + 2) * NG]], 1)
        product = field * jnp.concatenate([weight, weight], 0)
        back = dot3(to_k, split(product), (1, 0))
        for h in range(2):
            high, low = split(
                jnp.concatenate([back[:IXP, h * LP : (h + 1) * LP], back[IXP:, h * LP : (h + 1) * LP]], 1)
            )
            at = slice((z + h) * IXP, (z + h + 1) * IXP)
            sph[at], spl[at] = high, low

    out2 = []
    for pair in reversed(range(nz // 2)):
        offsets = ((nz - pair) % nz, pair + 1)
        owners = [lax.rem(me + offset, nz) for offset in offsets]
        phase = tuple(jnp.concatenate([b[:, block_lanes(q)] for q in owners], 1) for b in (bth, btl))
        hot = jnp.concatenate([mask[:, block_lanes(q)] for q in owners], 1)
        found = dot3((sph[...], spl[...]), phase, (1, 0))
        picked = jnp.sum(found.reshape(planes, IXP, 2 * lanes) * hot[None], axis=1)
        for place, (offset, q) in enumerate(zip(offsets, owners)):
            part = picked[:, place * lanes : (place + 1) * lanes]
            if offset == 0:
                recv2[me] = part
            else:
                send2[q] = part
                copy = transfer(send2, recv2, ssem2, rsem2, offset)
                copy.start()
                out2.append(copy)

    column = tabx[pl.ds(me, 1), :]
    mx, my = decode(column)
    fx = mx + kp_ref[0:1, 0:1]
    fy = my + kp_ref[0:1, 1:2]
    trans[NG:, :] = jnp.zeros((LP - NG, lanes), F32)
    trans[NG : NG + 1, :] = fx * fx + fy * fy
    trans[NG + 1 : NG + 2, :] = jnp.where(column < float(NG * NG), 1.0, 0.0)
    freq = lax.broadcasted_iota(jnp.int32, (1, NG), 1)
    fz = jnp.where(freq < NG // 2, freq, freq - NG).astype(F32) + kp_ref[0:1, 2:3]
    projector.finish_resident()
    projector.flatten_resident()
    for copy in out1:
        copy.wait_send()
    for copy in out2:
        copy.wait()
    trans[0:NG, :] = recv2[...].reshape(NG, lanes)
    turned = trans[...].T
    result = dot3(split(turned[: 2 * slots]), (zb[0], zb[1]), (1, 0))
    alive = turned[:slots, NG + 1 : NG + 2]
    kinetic = (KINETIC / (NG * NG)) * (turned[:slots, NG : NG + 1] + fz * fz) * alive
    images = (
        (result[:slots, :LP] + result[slots:, LP:])[:, :NG] + kinetic * wf_ref[0],
        (result[slots:, :LP] - result[:slots, LP:])[:, :NG] + kinetic * wf_ref[1],
    )
    projector.pack(images)
    for c in range(2):
        out_ref[c] = images[c]
    livecol[...] = jnp.broadcast_to(alive, livecol.shape)
    first_gram = projector.gather()
    projector.correct(projector.margin(first_gram))
    projector.scatter()
    for c in range(2):
        out_ref[c] = out_ref[c] - livecol[...] * projector.correction(c)


ORDER = (0, 1, 7, 2, 6, 3, 5, 4)


class Projector:
    def __init__(self, nz, slots, rows, refs):
        (self.res, self.dbuf, self.dh, self.dl, self.packed, self.abuf, self.ih, self.il, self.mpair, self.mall,
         self.cbuf, self.rbuf, self.fbuf, self.unpacked,
         self.dsem, self.psem, self.agsem, self.mpsem, self.mssem, self.mrsem, self.rssem, self.fsem) = refs
        self.nz, self.half, self.rows = nz, slots // 2, rows
        self.lines = self.half * NG // LP
        self.block = 2 * self.lines
        self.parts = ((0, 64), (64, self.block - 64))
        band = lax.axis_index("band")
        nb = 16
        self.me = lax.axis_index("plane")
        self.core = lax.rem(band, 2)
        self.partner = {"band": band + 1 - 2 * self.core}
        chip = band - self.core
        self.sides = (lax.rem(chip + 2, nb), lax.rem(chip + nb - 2, nb))

    def beside(self, way, core):
        return {"band": self.sides[way] + core}

    def remote(self, src, dst, send, recv, device):
        return pltpu.make_async_remote_copy(
            src_ref=src, dst_ref=dst, send_sem=send, recv_sem=recv, device_id=device, device_id_type=MESH
        )

    def greet(self, barrier):
        others = [self.beside(way, core) for way in range(2) for core in range(2)]
        for device in [self.partner] + others:
            pl.semaphore_signal(barrier, inc=1, device_id=device, device_id_type=MESH)
        return 5

    def slab(self, i):
        place = (self.core * self.rows * 2 + i) * self.half
        return self.dbuf.at[pl.ds(pl.multiple_of(place, 8), self.half), :]

    def local_fetch(self, i):
        own = pl.ds(pl.multiple_of(self.core * self.half, 8), self.half)
        return pltpu.make_async_copy(self.res.at[i, own, :], self.slab(i), self.dsem.at[0, i])

    def swap_resident(self, i):
        other = pl.ds(pl.multiple_of((1 - self.core) * self.half, 8), self.half)
        return self.remote(
            self.res.at[i, other, :], self.slab(i), self.dsem.at[1, i], self.dsem.at[2, i], self.partner
        )

    def start_resident(self):
        @pl.loop(0, 2 * self.rows)
        def _(i):
            self.swap_resident(i).start()
            self.local_fetch(i).start()

    def finish_resident(self):
        @pl.loop(0, 2 * self.rows)
        def _(i):
            self.swap_resident(i).wait()
            self.local_fetch(i).wait()

    def flatten_resident(self):
        third = self.lines // 3
        span = 2 * self.half

        @pl.loop(0, third)
        def _(i):
            for c in range(2):
                for group in range(2 * self.rows // 16):
                    base = group * 16 * span + c * self.half + i
                    tail = self.dbuf[pl.ds(base + self.lines, 16, stride=span), :]
                    for k in range(3):
                        head = self.dbuf[pl.ds(base + k * third, 16, stride=span), :]
                        line = jnp.concatenate([head, tail[:, k * 32 : (k + 1) * 32]], 1)
                        lanes = pl.ds(pl.multiple_of((k * third + i) * LP, LP), LP)
                        at = slice(c * 2 * self.rows + group * 16, c * 2 * self.rows + group * 16 + 16)
                        self.dh[at, lanes], self.dl[at, lanes] = split(line)

    def at(self, rel, sub, part=None):
        place = (ORDER.index(rel % 8) * 2 + sub) * self.block
        if part is None:
            return pl.ds(pl.multiple_of(place, 8), self.block)
        start, size = self.parts[part]
        return pl.ds(pl.multiple_of(place + start, 8), size)

    def pack(self, images):
        third = self.lines // 3
        for hh in range(2):
            for c in range(2):
                part = images[c][hh * self.half : (hh + 1) * self.half]
                self.packed[hh, c * self.lines : (c + 1) * self.lines, 0:NG] = part[: self.lines, :NG]
                for k in range(3):
                    start = c * self.lines + k * third
                    self.packed[hh, start : start + third, NG:LP] = part[self.lines :, k * 32 : (k + 1) * 32]

    def gather(self):
        mine, other = self.core, 1 - self.core
        pair = self.remote(
            self.packed.at[other], self.abuf.at[self.at(0, mine)], self.psem.at[0], self.psem.at[1], self.partner
        )
        sign = (-1, 1)

        def first(way, core, part):
            start, size = self.parts[part]
            return self.remote(
                self.packed.at[core, pl.ds(start, size)], self.abuf.at[self.at(sign[way], mine, part)],
                self.agsem.at[0, way, 0, core, part], self.agsem.at[1, way, 0, mine, part], self.beside(way, core),
            )

        def hop(way, step, sub, part):
            return self.remote(
                self.abuf.at[self.at(sign[way] * step, sub, part)],
                self.abuf.at[self.at(sign[way] * (step + 1), sub, part)],
                self.agsem.at[0, way, step, sub, part], self.agsem.at[1, way, step, sub, part],
                self.beside(way, mine),
            )

        started = [first(way, core, part) for part in range(2) for core in range(2) for way in range(2)]
        for copy in started:
            copy.start()
        pair.start()
        self.abuf[self.at(0, mine), :] = self.packed[mine]
        for step in (1, 2, 3):
            if step == 3:
                pair.wait()
                self.flatten_images(0)
            for part in range(2):
                for sub in range(2):
                    for way in range(2):
                        if step == 3 and sub != way:
                            continue
                        hop(way, step - 1, sub, part).wait_recv()
                        copy = hop(way, step, sub, part)
                        copy.start()
                        started.append(copy)
        first_gram = self.gram(0)
        for part in range(2):
            for way in range(2):
                hop(way, 2, 1 - way, part).wait_recv()
                hop(way, 3, way, part).wait_recv()
        for copy in started:
            copy.wait_send()
        return first_gram

    def flatten_images(self, group):
        @pl.loop(0, self.lines)
        def _(r):
            lanes = pl.ds(pl.multiple_of(r * LP, LP), LP)
            value = jnp.concatenate(
                [
                    self.abuf[pl.ds(group * 8 * self.block + c * self.lines + r, 8, stride=self.block), :]
                    for c in range(2)
                ],
                0,
            )
            self.ih[group, :, lanes], self.il[group, :, lanes] = split(value)

    def gram(self, group):
        count = 2 * self.rows
        gram = dot3((self.ih[group], self.il[group]), (self.dh[...], self.dl[...]), (1, 1))
        real = gram[:8, :count] + gram[8:, count:]
        imag = gram[8:, :count] - gram[:8, count:]
        return jnp.concatenate([real, imag], 1)

    def margin(self, first_gram):
        self.flatten_images(1)
        count = 2 * self.rows
        self.mpair[0] = jnp.concatenate([first_gram, self.gram(1)], 1)
        swap = self.remote(self.mpair.at[0], self.mpair.at[1], self.mpsem.at[0], self.mpsem.at[1], self.partner)
        swap.start()
        swap.wait()
        self.mall[self.me] = self.mpair[0] + self.mpair[1]
        copies = []
        for step in sorted(range(1, self.nz), key=lambda i: -min(i, self.nz - i)):
            copy = self.remote(
                self.mall.at[self.me], self.mall.at[self.me],
                self.mssem.at[step], self.mrsem.at[step], {"plane": lax.rem(self.me + step, self.nz)},
            )
            copy.start()
            copies.append(copy)
        for copy in copies:
            copy.wait()
        flat = jnp.sum(self.mall[...], axis=0)
        both = jnp.concatenate([flat[:, : 2 * count], flat[:, 2 * count :]], 0)
        real, imag = both[:, :count], both[:, count:]
        return jnp.concatenate(
            [jnp.concatenate([real, -imag], 1), jnp.concatenate([imag, real], 1)], 0
        )

    def correct(self, margin):
        left = split(margin)
        batch = 4

        @pl.loop(0, self.lines // batch)
        def _(g):
            lanes = pl.ds(pl.multiple_of(g * batch * LP, LP), batch * LP)
            value = dot3(left, (self.dh[:, lanes], self.dl[:, lanes]), (1, 0))
            for i in range(batch):
                for c in range(2):
                    self.cbuf[pl.ds(c * self.lines + g * batch + i, 16, stride=self.block), :] = value[
                        c * 16 : (c + 1) * 16, i * LP : (i + 1) * LP
                    ]

    def scatter(self):
        mine, other = self.core, 1 - self.core

        def slot(way, k, sub, part=None):
            place = ((way * 4 + k) * 2 + sub) * self.block
            start, size = (0, self.block) if part is None else self.parts[part]
            return pl.ds(pl.multiple_of(place + start, 8), size)

        def own(way, k, sub, part):
            return self.at(k if way == 0 else -k, sub, part)

        def hop(way, k, sub, part, source):
            if k == 1:
                target, device = mine, self.beside(way, sub)
            else:
                target, device = sub, self.beside(way, mine)
            return self.remote(
                source, self.rbuf.at[slot(way, k - 1, target, part)],
                self.rssem.at[0, way, k - 1, sub, part], self.rssem.at[1, way, k - 1, target, part], device,
            )

        def arrived(way, k, index, part):
            here = self.rbuf.at[slot(way, k, index, part)]
            return self.remote(
                here, here, self.rssem.at[0, way, k, index, part], self.rssem.at[1, way, k, index, part],
                self.beside(way, mine),
            )

        sent = []
        for k in (4, 3, 2, 1):
            for part in range(2):
                for sub in range(2):
                    for way in range(2):
                        first = 4 if sub == way else 3
                        if k > first:
                            continue
                        source = self.cbuf.at[own(way, k, sub, part)]
                        if k < first:
                            arrived(way, k, sub, part).wait_recv()
                            here = slot(way, k, sub, part)
                            self.rbuf[here, :] = self.rbuf[here, :] + self.cbuf[own(way, k, sub, part), :]
                            source = self.rbuf.at[here]
                        copy = hop(way, k, sub, part, source)
                        copy.start()
                        sent.append(copy)
            if k == 3:
                copy = self.remote(
                    self.cbuf.at[self.at(0, other)], self.fbuf.at[2], self.fsem.at[0], self.fsem.at[1], self.partner
                )
                copy.start()
        for part in range(2):
            for index in range(2):
                for way in range(2):
                    arrived(way, 0, index, part).wait_recv()
        arrivals = [self.rbuf[slot(0, 0, half), :] + self.rbuf[slot(1, 0, half), :] for half in (mine, other)]
        self.fbuf[0] = self.cbuf[self.at(0, mine), :] + arrivals[0]
        self.finish_pair(other)
        self.fbuf[1] = self.fbuf[2] + arrivals[1]
        for copy in sent:
            copy.wait_send()
        self.unpack(0, mine)
        self.unpack(1, other)

    def finish_pair(self, other):
        self.remote(
            self.cbuf.at[self.at(0, other)], self.fbuf.at[2], self.fsem.at[0], self.fsem.at[1], self.partner
        ).wait()

    def unpack(self, source, hh):
        third = self.lines // 3
        for c in range(2):
            start = c * self.lines
            self.unpacked[hh, c, 0 : self.lines, :] = self.fbuf[source, start : start + self.lines, 0:NG]
            for k in range(3):
                self.unpacked[hh, c, self.lines : self.half, k * 32 : (k + 1) * 32] = self.fbuf[
                    source, start + k * third : start + (k + 1) * third, NG:LP
                ]

    def correction(self, c):
        return jnp.concatenate([self.unpacked[0, c], self.unpacked[1, c]], 0)

    @staticmethod
    def scratch(nz, slots, rows):
        half = slots // 2
        lines = half * NG // LP
        block = 2 * lines
        dma = pltpu.SemaphoreType.DMA
        return [
            pltpu.VMEM((4 * rows * half, NG), F32),
            pltpu.VMEM((4 * rows, lines * LP), BF16),
            pltpu.VMEM((4 * rows, lines * LP), BF16),
            pltpu.VMEM((2, block, LP), F32),
            pltpu.VMEM((16 * block, LP), F32),
            pltpu.VMEM((2, 16, lines * LP), BF16),
            pltpu.VMEM((2, 16, lines * LP), BF16),
            pltpu.VMEM((2, 8, LP), F32),
            pltpu.VMEM((nz, 8, LP), F32),
            pltpu.VMEM((16 * block, LP), F32),
            pltpu.VMEM((16 * block, LP), F32),
            pltpu.VMEM((3, block, LP), F32),
            pltpu.VMEM((2, 2, half, NG), F32),
            dma((3, 2 * rows)), dma((2,)), dma((2, 2, 4, 2, 2)), dma((2,)), dma((nz,)), dma((nz,)), dma((2, 2, 4, 2, 2)), dma((2,)),
        ]


def kernel(nz, slots, planes, rows, *refs):
    inputs, resident, out_ref, rest = refs[:9], refs[9], refs[10], refs[11:]
    count = 30
    projector = Projector(nz, slots, rows, (resident,) + rest[count:])
    local_kernel(nz, slots, planes, inputs, out_ref, *rest[:count], projector=projector)


def on_device(wavefunctions, resident, potential, stick_column_table, kpoint, nz):
    slots = wavefunctions.shape[3]
    planes = potential.shape[0]
    rows = resident.shape[1]
    lanes = -(-2 * slots // LP) * LP
    consts = [jnp.asarray(t) for t in tables()]
    block = pltpu.VMEM((nz, planes, lanes), F32)
    dma = pltpu.SemaphoreType.DMA
    operands = (wavefunctions[0, 0], stick_column_table, potential, kpoint, *consts)
    out = pl.pallas_call(
        functools.partial(kernel, nz, slots, planes, rows),
        out_shape=jax.ShapeDtypeStruct((2, slots, NG), F32),
        in_specs=[pl.BlockSpec(memory_space=pl.ANY)] * 10,
        out_specs=pl.BlockSpec(memory_space=pltpu.VMEM),
        scratch_shapes=[pltpu.VMEM(x.shape, x.dtype) for x in operands]
        + [
            dma((9,)),
            block, block, block, block,
            pltpu.VMEM((2 * LP, nz * lanes), BF16),
            pltpu.VMEM((2 * LP, nz * lanes), BF16),
            pltpu.VMEM((2, planes * IXP, 2 * lanes), BF16),
            pltpu.VMEM((2, planes * IXP, 2 * lanes), BF16),
            pltpu.VMEM((IXP, nz * lanes), F32),
            pltpu.VMEM((planes * IXP, 2 * LP), F32),
            pltpu.VMEM((planes * IXP, 2 * LP), BF16),
            pltpu.VMEM((planes * IXP, 2 * LP), BF16),
            pltpu.VMEM((16, lanes), F32),
            pltpu.VMEM((planes * NG, LP), F32),
            pltpu.VMEM((LP, lanes), F32),
            pltpu.VMEM((slots, NG), F32),
            dma((nz,)), dma((nz,)), dma((nz,)), dma((nz,)),
        ]
        + Projector.scratch(nz, slots, rows),
        compiler_params=pltpu.CompilerParams(collective_id=0, has_side_effects=True),
    )(*operands, resident[0].reshape(2 * rows, slots, NG))
    return out[None, None]


def solution(mesh):
    in_specs = (
        P("kpt", "band", None, "plane", None),
        P("kpt", "band", None, "plane", None),
        P("plane", None),
        P("kpt", None),
        P("kpt", None),
    )
    out_specs = P("kpt", "band", None, "plane", None)
    return jax.shard_map(
        functools.partial(on_device, nz=mesh.shape["plane"]),
        mesh=mesh, in_specs=in_specs, out_specs=out_specs, check_vma=False,
    )
```

```python
import functools
import math

import jax
import jax.numpy as jnp
import numpy as np
from jax import lax
from jax.experimental import pallas as pl
from jax.experimental.pallas import tpu as pltpu
from jax.sharding import PartitionSpec as P

NG = 96
KINETIC = 12.0
HIGHEST = lax.Precision.HIGHEST
MESH = pl.DeviceIdType.MESH
RAD = NG // 4
TAIL = 32
SIZES = (32, 32, 16)
STARTS = (0, 32, 64)
LINES = (24, 24, 12)
FIRSTS = (0, 24, 48)
IXP = 64
LP = 128
F32 = jnp.float32
BF16 = jnp.bfloat16


def split_np(table):
    table = np.asarray(table, np.float32)
    high = table.astype(jnp.bfloat16)
    low = (table - high.astype(np.float32)).astype(jnp.bfloat16)
    return high, low


def tables():
    turn = 2.0 * math.pi / NG
    grid = np.arange(NG)
    full = np.outer(grid, grid) % NG * turn
    tz = np.concatenate([np.cos(full), np.sin(full)], axis=0)
    signed = np.arange(IXP) - RAD
    inside = (np.arange(IXP) <= 2 * RAD).astype(np.float64)
    part = np.outer(grid, signed) % NG * turn
    cosine = np.cos(part) * inside
    sine = np.sin(part) * inside
    pad = np.zeros((LP - NG, IXP))
    cy = np.concatenate([cosine, pad])
    sy = np.concatenate([sine, pad])
    ty = np.block([[cy, -sy], [sy, cy]])
    xf = np.block([[cosine, -sine], [sine, cosine]])
    xb = np.block([[cosine.T, sine.T], [-sine.T, cosine.T]]) / float(NG) ** 3
    zb = np.zeros((LP, 2 * LP))
    zb[:NG, :NG] = np.cos(full)
    zb[:NG, LP : LP + NG] = np.sin(full)
    return [np.stack(split_np(table)) for table in (tz, ty, xf, xb, zb)]


def split(value):
    high = value.astype(BF16)
    low = (value - high.astype(F32)).astype(BF16)
    return high, low


def dot3(left, right, axes):
    dims = (((axes[0],), (axes[1],)), ((), ()))

    def one(a, b):
        return lax.dot_general(a, b, dims, preferred_element_type=F32)

    return one(left[0], right[0]) + (one(left[1], right[0]) + one(left[0], right[1]))


def pieces(slots):
    for t, (size, start) in enumerate(zip(SIZES, STARTS)):
        for c in range(2):
            for h in range(2):
                yield c, h, t * LP + (c * 2 + h) * size, size, h * (slots // 2) + start


def local_kernel(
    nz, slots, planes,
    inputs, out_ref,
    wf_ref, table_ref, pot_ref, kp_ref, tz, ty, xf, xb, zb, insem,
    send1, recv1, send2, recv2, bth, btl, lhh, lhl, mask, acc, sph, spl, tabx, weights, trans, livecol,
    ssem1, rsem1, ssem2, rsem2,
    projector,
):
    me = lax.axis_index("plane")
    lanes = send1.shape[2]
    barrier = pltpu.get_barrier_semaphore()
    for step in range(1, nz):
        pl.semaphore_signal(barrier, inc=1, device_id={"plane": lax.rem(me + step, nz)}, device_id_type=MESH)
    greeted = projector.greet(barrier)
    held = (wf_ref, table_ref, pot_ref, kp_ref, tz, ty, xf, xb, zb)
    fetches = [pltpu.make_async_copy(a, b, insem.at[i]) for i, (a, b) in enumerate(zip(inputs, held))]
    for i in (0, 4, 1, 5, 2, 3, 6, 7, 8):
        fetches[i].start()
    fetches[0].wait()
    fetches[4].wait()

    forward = (tz[0], tz[1])
    from_real = dot3(forward, split(wf_ref[0]), (1, 1))
    from_imag = dot3(forward, split(wf_ref[1]), (1, 1))
    real = from_real[:NG] - from_imag[NG:]
    imag = from_imag[:NG] + from_real[NG:]
    for c, h, lane, size, slot in pieces(slots):
        part = (real, imag)[c][:, slot : slot + size]
        send1[:, :, lane : lane + size] = part.reshape(nz, planes, size)
    send1[:, :, 2 * slots :] = jnp.zeros((nz, planes, lanes - 2 * slots), F32)
    pl.semaphore_wait(barrier, nz - 1 + greeted)

    def transfer(source, target, ssem, rsem, step):
        there = lax.rem(me + step, nz)
        return pltpu.make_async_remote_copy(
            src_ref=source.at[there],
            dst_ref=target.at[me],
            send_sem=ssem.at[step],
            recv_sem=rsem.at[step],
            device_id={"plane": there},
            device_id_type=MESH,
        )

    out1 = [transfer(send1, recv1, ssem1, rsem1, step) for step in range(1, nz)]
    for step in sorted(range(1, nz), key=lambda i: -min(i, nz - i)):
        out1[step - 1].start()
    projector.start_resident()
    for i in (1, 5, 2, 3, 6, 7, 8):
        fetches[i].wait()

    tabx[...] = jnp.full(tabx.shape, float(NG * NG), F32)
    columns = table_ref[...].astype(F32)
    for q in range(nz):
        for c, h, lane, size, slot in pieces(slots):
            tabx[q : q + 1, lane : lane + size] = columns[:, q * slots + slot : q * slots + slot + size]

    def decode(column):
        ix = ((column + 0.5) * (1.0 / NG)).astype(jnp.int32).astype(F32)
        iy = column - ix * NG
        return jnp.where(ix < NG // 2, ix, ix - NG), jnp.where(iy < NG // 2, iy, iy - NG)

    def block_lanes(q):
        return pl.ds(pl.multiple_of(q * lanes, LP), lanes)

    lane = lax.broadcasted_iota(jnp.int32, (1, lanes), 1)
    inner = jnp.where(lane < LP, lane, jnp.where(lane < 2 * LP, lane - LP, 2 * (lane - 2 * LP)))
    second = inner >= LP // 2
    rows = lax.broadcasted_iota(jnp.int32, (2 * IXP, lanes), 0).astype(F32)

    @pl.loop(0, nz)
    def _(q):
        column = tabx[pl.ds(q, 1), :]
        alive = column < float(NG * NG)
        mx, my = decode(column)
        kx = jnp.where(alive, mx + RAD, -1.0)
        ky = jnp.where(alive, my + RAD + jnp.where(second, float(IXP), 0.0), -1.0)
        mask[:, block_lanes(q)] = jnp.where(rows[:IXP] == kx, 1.0, 0.0)
        hot = jnp.where(rows == ky, 1.0, 0.0).astype(BF16)
        for i, into in ((0, bth), (1, btl)):
            into[:, block_lanes(q)] = jnp.dot(ty[i], hot, preferred_element_type=F32).astype(BF16)

    zeros = jnp.zeros((weights.shape[0], LP - NG), F32)
    weights[:, NG:LP] = zeros
    for x in range(NG):
        weights[pl.ds(x, planes, stride=NG), 0:NG] = pot_ref[:, x * NG : (x + 1) * NG]

    for pair in range(nz // 2):
        offsets = ((nz - pair) % nz, pair + 1)
        owners = [lax.rem(me + offset, nz) for offset in offsets]
        side = pair % 2
        for place, (offset, q) in enumerate(zip(offsets, owners)):
            if offset == 0:
                values = send1[me]
            else:
                out1[(nz - offset) - 1].wait_recv()
                values = recv1[q]
            hot = mask[:, block_lanes(q)].astype(BF16)
            into = slice(place * lanes, (place + 1) * lanes)
            for z in range(planes):
                high, low = split(jnp.broadcast_to(values[z : z + 1], (16, lanes)))
                for g in range(IXP // 16):
                    part = hot[g * 16 : (g + 1) * 16]
                    at = slice(z * IXP + g * 16, z * IXP + (g + 1) * 16)
                    lhh[side, at, into] = part * high
                    lhl[side, at, into] = part * low
        phase = tuple(jnp.concatenate([b[:, block_lanes(q)] for q in owners], 1) for b in (bth, btl))
        term = dot3((lhh[side], lhl[side]), phase, (1, 1))
        acc[...] = term if pair == 0 else acc[...] + term

    to_x = (xf[0], xf[1])
    to_k = (xb[0], xb[1])
    for z in range(0, planes, 2):
        a = acc[z * IXP : (z + 1) * IXP]
        b = acc[(z + 1) * IXP : (z + 2) * IXP]
        joined = jnp.concatenate(
            [jnp.concatenate([a[:, :LP], b[:, :LP]], 1), jnp.concatenate([a[:, LP:], b[:, LP:]], 1)], 0
        )
        field = dot3(to_x, split(joined), (1, 0))
        weight = jnp.concatenate([weights[z * NG : (z + 1) * NG], weights[(z + 1) * NG : (z + 2) * NG]], 1)
        product = field * jnp.concatenate([weight, weight], 0)
        back = dot3(to_k, split(product), (1, 0))
        for h in range(2):
            high, low = split(
                jnp.concatenate([back[:IXP, h * LP : (h + 1) * LP], back[IXP:, h * LP : (h + 1) * LP]], 1)
            )
            at = slice((z + h) * IXP, (z + h + 1) * IXP)
            sph[at], spl[at] = high, low

    def returning(t, offset):
        there = lax.rem(me + offset, nz)
        return pltpu.make_async_remote_copy(
            src_ref=send2.at[t, there],
            dst_ref=recv2.at[t, me],
            send_sem=ssem2.at[t, offset],
            recv_sem=rsem2.at[t, offset],
            device_id={"plane": there},
            device_id_type=MESH,
        )

    chunks = len(SIZES)
    for t in range(chunks):
        for pair in reversed(range(nz // 2)):
            offsets = ((nz - pair) % nz, pair + 1)
            owners = [lax.rem(me + offset, nz) for offset in offsets]
            tiles = [pl.ds(pl.multiple_of(q * lanes + t * LP, LP), LP) for q in owners]
            phase = tuple(jnp.concatenate([b[:, tile] for tile in tiles], 1) for b in (bth, btl))
            hot = jnp.concatenate([mask[:, tile] for tile in tiles], 1)
            found = dot3((sph[...], spl[...]), phase, (1, 0))
            picked = jnp.sum(found.reshape(planes, IXP, 2 * LP) * hot[None], axis=1)
            for place, (offset, q) in enumerate(zip(offsets, owners)):
                part = picked[:, place * LP : (place + 1) * LP]
                if offset == 0:
                    recv2[t, me] = part
                else:
                    send2[t, q] = part
                    returning(t, offset).start()

    column = tabx[pl.ds(me, 1), :]
    mx, my = decode(column)
    fx = mx + kp_ref[0:1, 0:1]
    fy = my + kp_ref[0:1, 1:2]
    trans[NG:, :] = jnp.zeros((LP - NG, lanes), F32)
    trans[NG : NG + 1, :] = fx * fx + fy * fy
    trans[NG + 1 : NG + 2, :] = jnp.where(column < float(NG * NG), 1.0, 0.0)
    freq = lax.broadcasted_iota(jnp.int32, (1, NG), 1)
    fz = jnp.where(freq < NG // 2, freq, freq - NG).astype(F32) + kp_ref[0:1, 2:3]
    projector.finish_resident()
    projector.flatten_resident()
    for copy in out1:
        copy.wait_send()

    def images_of(t):
        for offset in range(1, nz):
            returning(t, offset).wait_recv()
        tile = slice(t * LP, (t + 1) * LP)
        trans[0:NG, tile] = recv2[t].reshape(NG, LP)
        turned = trans[:, tile].T
        result = dot3(split(turned), (zb[0], zb[1]), (1, 0))
        size, start = SIZES[t], STARTS[t]
        upper, lower = result[: 2 * size], result[2 * size : 4 * size]
        alive = turned[: 2 * size, NG + 1 : NG + 2]
        kinetic = (KINETIC / (NG * NG)) * (turned[: 2 * size, NG : NG + 1] + fz * fz) * alive
        spots = [slice(h * (slots // 2) + start, h * (slots // 2) + start + size) for h in range(2)]
        own = [jnp.concatenate([wf_ref[c, spot] for spot in spots], 0) for c in range(2)]
        images = (
            (upper[:, :LP] + lower[:, LP:])[:, :NG] + kinetic * own[0],
            (lower[:, :LP] - upper[:, LP:])[:, :NG] + kinetic * own[1],
        )
        wide = jnp.broadcast_to(alive, (2 * size, NG))
        for h, spot in enumerate(spots):
            for c in range(2):
                out_ref[c, spot] = images[c][h * size : (h + 1) * size]
            livecol[spot] = wide[h * size : (h + 1) * size]
        projector.pack(images, t)

    first_gram = projector.gather(images_of)
    projector.scatter(projector.margin(first_gram))
    for t in range(chunks):
        for offset in range(1, nz):
            returning(t, offset).wait_send()
    for c in range(2):
        out_ref[c] = out_ref[c] - livecol[...] * projector.correction(c)


ORDER = (0, 1, 7, 2, 6, 3, 5, 4)


class Projector:
    def __init__(self, nz, slots, rows, refs):
        (self.res, self.dbuf, self.dh, self.dl, self.packed, self.abuf, self.ih, self.il, self.mpair, self.mall,
         self.cbuf, self.rbuf, self.fbuf, self.unpacked,
         self.dsem, self.psem, self.agsem, self.mpsem, self.mssem, self.mrsem, self.rssem, self.fsem) = refs
        self.nz, self.half, self.rows = nz, slots // 2, rows
        self.lines = self.half * NG // LP
        self.block = 2 * self.lines
        self.parts = tuple((2 * first, 2 * count) for first, count in zip(FIRSTS, LINES))
        band = lax.axis_index("band")
        nb = 16
        self.me = lax.axis_index("plane")
        self.core = lax.rem(band, 2)
        self.partner = {"band": band + 1 - 2 * self.core}
        chip = band - self.core
        self.sides = (lax.rem(chip + 2, nb), lax.rem(chip + nb - 2, nb))

    def beside(self, way, core):
        return {"band": self.sides[way] + core}

    def remote(self, src, dst, send, recv, device):
        return pltpu.make_async_remote_copy(
            src_ref=src, dst_ref=dst, send_sem=send, recv_sem=recv, device_id=device, device_id_type=MESH
        )

    def greet(self, barrier):
        others = [self.beside(way, core) for way in range(2) for core in range(2)]
        for device in [self.partner] + others:
            pl.semaphore_signal(barrier, inc=1, device_id=device, device_id_type=MESH)
        return 5

    def slab(self, i):
        place = (self.core * self.rows * 2 + i) * self.half
        return self.dbuf.at[pl.ds(pl.multiple_of(place, 8), self.half), :]

    def local_fetch(self, i):
        own = pl.ds(pl.multiple_of(self.core * self.half, 8), self.half)
        return pltpu.make_async_copy(self.res.at[i, own, :], self.slab(i), self.dsem.at[0, i])

    def swap_resident(self, i):
        other = pl.ds(pl.multiple_of((1 - self.core) * self.half, 8), self.half)
        return self.remote(
            self.res.at[i, other, :], self.slab(i), self.dsem.at[1, i], self.dsem.at[2, i], self.partner
        )

    def start_resident(self):
        @pl.loop(0, 2 * self.rows)
        def _(i):
            self.swap_resident(i).start()
            self.local_fetch(i).start()

    def finish_resident(self):
        @pl.loop(0, 2 * self.rows)
        def _(i):
            self.swap_resident(i).wait()
            self.local_fetch(i).wait()

    def flatten_resident(self):
        span = 2 * self.half
        for t, (count, first, slot) in enumerate(zip(LINES, FIRSTS, STARTS)):
            third = count // 3

            @pl.loop(0, third)
            def _(i):
                for c in range(2):
                    for group in range(2 * self.rows // 16):
                        base = group * 16 * span + c * self.half + slot + i
                        tail = self.dbuf[pl.ds(base + count, 16, stride=span), :]
                        for k in range(3):
                            head = self.dbuf[pl.ds(base + k * third, 16, stride=span), :]
                            line = jnp.concatenate([head, tail[:, k * TAIL : (k + 1) * TAIL]], 1)
                            lanes = pl.ds(pl.multiple_of((first + k * third + i) * LP, LP), LP)
                            at = slice(c * 2 * self.rows + group * 16, c * 2 * self.rows + group * 16 + 16)
                            self.dh[at, lanes], self.dl[at, lanes] = split(line)

    def at(self, rel, sub, part=None):
        place = (ORDER.index(rel % 8) * 2 + sub) * self.block
        if part is None:
            return pl.ds(pl.multiple_of(place, 8), self.block)
        start, size = self.parts[part]
        return pl.ds(pl.multiple_of(place + start, 8), size)

    def pack(self, images, t):
        size, count = SIZES[t], LINES[t]
        third = count // 3
        for hh in range(2):
            for c in range(2):
                part = images[c][hh * size : (hh + 1) * size]
                base = self.parts[t][0] + c * count
                self.packed[hh, base : base + count, 0:NG] = part[:count]
                for k in range(3):
                    self.packed[hh, base + k * third : base + (k + 1) * third, NG:LP] = part[
                        count:, k * TAIL : (k + 1) * TAIL
                    ]

    def gather(self, images_of):
        mine, other = self.core, 1 - self.core
        sign = (-1, 1)

        def rows(part):
            start, size = self.parts[part]
            return pl.ds(start, size)

        def pair(part):
            return self.remote(
                self.packed.at[other, rows(part)], self.abuf.at[self.at(0, mine, part)],
                self.psem.at[0, part], self.psem.at[1, part], self.partner,
            )

        def first(way, core, part):
            return self.remote(
                self.packed.at[core, rows(part)], self.abuf.at[self.at(sign[way], mine, part)],
                self.agsem.at[0, way, 0, core, part], self.agsem.at[1, way, 0, mine, part], self.beside(way, core),
            )

        def hop(way, step, sub, part):
            return self.remote(
                self.abuf.at[self.at(sign[way] * step, sub, part)],
                self.abuf.at[self.at(sign[way] * (step + 1), sub, part)],
                self.agsem.at[0, way, step, sub, part], self.agsem.at[1, way, step, sub, part],
                self.beside(way, mine),
            )

        started = []
        for step, part in (
            (0, 0), (0, 1), (1, 0), (0, 2), (1, 1), (2, 0), (1, 2), (2, 1), (3, 0), (2, 2), (3, 1), (3, 2)
        ):
            if step == 0:
                images_of(part)
                for core in range(2):
                    for way in range(2):
                        started.append(first(way, core, part))
                        started[-1].start()
                pair(part).start()
                self.abuf[self.at(0, mine, part), :] = self.packed[mine, rows(part)]
                continue
            for sub in range(2):
                for way in range(2):
                    if step == 3 and sub != way:
                        continue
                    hop(way, step - 1, sub, part).wait_recv()
                    started.append(hop(way, step, sub, part))
                    started[-1].start()
        for part in range(len(self.parts)):
            pair(part).wait()
        self.flatten_images(0)
        first_gram = self.gram(0)
        for part in range(len(self.parts)):
            for way in range(2):
                hop(way, 2, 1 - way, part).wait_recv()
                hop(way, 3, way, part).wait_recv()
        for copy in started:
            copy.wait_send()
        return first_gram

    def flatten_images(self, group):
        for (row, _), count, first in zip(self.parts, LINES, FIRSTS):

            @pl.loop(0, count)
            def _(r):
                lanes = pl.ds(pl.multiple_of((first + r) * LP, LP), LP)
                base = group * 8 * self.block + row + r
                value = jnp.concatenate(
                    [self.abuf[pl.ds(base + c * count, 8, stride=self.block), :] for c in range(2)], 0
                )
                self.ih[group, :, lanes], self.il[group, :, lanes] = split(value)

    def gram(self, group):
        count = 2 * self.rows
        gram = dot3((self.ih[group], self.il[group]), (self.dh[...], self.dl[...]), (1, 1))
        real = gram[:8, :count] + gram[8:, count:]
        imag = gram[8:, :count] - gram[:8, count:]
        return jnp.concatenate([real, imag], 1)

    def margin(self, first_gram):
        self.flatten_images(1)
        count = 2 * self.rows
        self.mpair[0] = jnp.concatenate([first_gram, self.gram(1)], 1)
        swap = self.remote(self.mpair.at[0], self.mpair.at[1], self.mpsem.at[0], self.mpsem.at[1], self.partner)
        swap.start()
        swap.wait()
        self.mall[self.me] = self.mpair[0] + self.mpair[1]
        copies = []
        for step in sorted(range(1, self.nz), key=lambda i: -min(i, self.nz - i)):
            copy = self.remote(
                self.mall.at[self.me], self.mall.at[self.me],
                self.mssem.at[step], self.mrsem.at[step], {"plane": lax.rem(self.me + step, self.nz)},
            )
            copy.start()
            copies.append(copy)
        for copy in copies:
            copy.wait()
        flat = jnp.sum(self.mall[...], axis=0)
        both = jnp.concatenate([flat[:, : 2 * count], flat[:, 2 * count :]], 0)
        real, imag = both[:, :count], both[:, count:]
        return jnp.concatenate(
            [jnp.concatenate([real, -imag], 1), jnp.concatenate([imag, real], 1)], 0
        )

    def correct(self, left, t):
        batch = 4
        count, first, row = LINES[t], FIRSTS[t], self.parts[t][0]

        @pl.loop(0, count // batch)
        def _(g):
            lanes = pl.ds(pl.multiple_of((first + g * batch) * LP, LP), batch * LP)
            value = dot3(left, (self.dh[:, lanes], self.dl[:, lanes]), (1, 0))
            for i in range(batch):
                for c in range(2):
                    self.cbuf[pl.ds(row + c * count + g * batch + i, 16, stride=self.block), :] = value[
                        c * 16 : (c + 1) * 16, i * LP : (i + 1) * LP
                    ]

    def scatter(self, margin):
        left = split(margin)
        mine, other = self.core, 1 - self.core

        def slot(way, k, sub, part=None):
            place = ((way * 4 + k) * 2 + sub) * self.block
            start, size = (0, self.block) if part is None else self.parts[part]
            return pl.ds(pl.multiple_of(place + start, 8), size)

        def own(way, k, sub, part):
            return self.at(k if way == 0 else -k, sub, part)

        def hop(way, k, sub, part, source):
            if k == 1:
                target, device = mine, self.beside(way, sub)
            else:
                target, device = sub, self.beside(way, mine)
            return self.remote(
                source, self.rbuf.at[slot(way, k - 1, target, part)],
                self.rssem.at[0, way, k - 1, sub, part], self.rssem.at[1, way, k - 1, target, part], device,
            )

        def arrived(way, k, index, part):
            here = self.rbuf.at[slot(way, k, index, part)]
            return self.remote(
                here, here, self.rssem.at[0, way, k, index, part], self.rssem.at[1, way, k, index, part],
                self.beside(way, mine),
            )

        sent = []

        def send(way, k, sub, part, source):
            sent.append(hop(way, k, sub, part, source))
            sent[-1].start()

        parts = range(len(self.parts))
        for part in parts:
            self.correct(left, part)
            for sub in range(2):
                for way in range(2):
                    k = 4 if sub == way else 3
                    send(way, k, sub, part, self.cbuf.at[own(way, k, sub, part)])
        self.remote(
            self.cbuf.at[self.at(0, other)], self.fbuf.at[2], self.fsem.at[0], self.fsem.at[1], self.partner
        ).start()
        for k in (3, 2, 1):
            for part in parts:
                for sub in range(2):
                    for way in range(2):
                        if k == 3 and sub != way:
                            continue
                        arrived(way, k, sub, part).wait_recv()
                        here = slot(way, k, sub, part)
                        self.rbuf[here, :] = self.rbuf[here, :] + self.cbuf[own(way, k, sub, part), :]
                        send(way, k, sub, part, self.rbuf.at[here])
        self.finish_pair(other)
        for part in parts:
            rows = pl.ds(*self.parts[part])
            for index in range(2):
                for way in range(2):
                    arrived(way, 0, index, part).wait_recv()
            for index, half, base in (
                (0, mine, self.cbuf[self.at(0, mine, part), :]), (1, other, self.fbuf[2, rows])
            ):
                self.fbuf[index, rows] = base + (
                    self.rbuf[slot(0, 0, half, part), :] + self.rbuf[slot(1, 0, half, part), :]
                )
                self.unpack(index, half, part)
        for copy in sent:
            copy.wait_send()

    def finish_pair(self, other):
        self.remote(
            self.cbuf.at[self.at(0, other)], self.fbuf.at[2], self.fsem.at[0], self.fsem.at[1], self.partner
        ).wait()

    def unpack(self, source, hh, t):
        count, slot = LINES[t], STARTS[t]
        third = count // 3
        for c in range(2):
            base = self.parts[t][0] + c * count
            self.unpacked[hh, c, slot : slot + count, :] = self.fbuf[source, base : base + count, 0:NG]
            for k in range(3):
                self.unpacked[hh, c, slot + count : slot + count + third, k * TAIL : (k + 1) * TAIL] = self.fbuf[
                    source, base + k * third : base + (k + 1) * third, NG:LP
                ]

    def correction(self, c):
        return jnp.concatenate([self.unpacked[0, c], self.unpacked[1, c]], 0)

    @staticmethod
    def scratch(nz, slots, rows):
        half = slots // 2
        lines = half * NG // LP
        block = 2 * lines
        dma = pltpu.SemaphoreType.DMA
        return [
            pltpu.VMEM((4 * rows * half, NG), F32),
            pltpu.VMEM((4 * rows, lines * LP), BF16),
            pltpu.VMEM((4 * rows, lines * LP), BF16),
            pltpu.VMEM((2, block, LP), F32),
            pltpu.VMEM((16 * block, LP), F32),
            pltpu.VMEM((2, 16, lines * LP), BF16),
            pltpu.VMEM((2, 16, lines * LP), BF16),
            pltpu.VMEM((2, 8, LP), F32),
            pltpu.VMEM((nz, 8, LP), F32),
            pltpu.VMEM((16 * block, LP), F32),
            pltpu.VMEM((16 * block, LP), F32),
            pltpu.VMEM((3, block, LP), F32),
            pltpu.VMEM((2, 2, half, NG), F32),
            dma((3, 2 * rows)), dma((2, 3)), dma((2, 2, 4, 2, 3)), dma((2,)), dma((nz,)), dma((nz,)), dma((2, 2, 4, 2, 3)), dma((2,)),
        ]


def kernel(nz, slots, planes, rows, *refs):
    inputs, resident, out_ref, rest = refs[:9], refs[9], refs[10], refs[11:]
    count = 30
    projector = Projector(nz, slots, rows, (resident,) + rest[count:])
    local_kernel(nz, slots, planes, inputs, out_ref, *rest[:count], projector=projector)


def on_device(wavefunctions, resident, potential, stick_column_table, kpoint, nz):
    slots = wavefunctions.shape[3]
    planes = potential.shape[0]
    rows = resident.shape[1]
    lanes = -(-2 * slots // LP) * LP
    consts = [jnp.asarray(t) for t in tables()]
    block = pltpu.VMEM((nz, planes, lanes), F32)
    dma = pltpu.SemaphoreType.DMA
    operands = (wavefunctions[0, 0], stick_column_table, potential, kpoint, *consts)
    out = pl.pallas_call(
        functools.partial(kernel, nz, slots, planes, rows),
        out_shape=jax.ShapeDtypeStruct((2, slots, NG), F32),
        in_specs=[pl.BlockSpec(memory_space=pl.ANY)] * 10,
        out_specs=pl.BlockSpec(memory_space=pltpu.VMEM),
        scratch_shapes=[pltpu.VMEM(x.shape, x.dtype) for x in operands]
        + [
            dma((9,)),
            block, block,
            pltpu.VMEM((3, nz, planes, LP), F32),
            pltpu.VMEM((3, nz, planes, LP), F32),
            pltpu.VMEM((2 * LP, nz * lanes), BF16),
            pltpu.VMEM((2 * LP, nz * lanes), BF16),
            pltpu.VMEM((2, planes * IXP, 2 * lanes), BF16),
            pltpu.VMEM((2, planes * IXP, 2 * lanes), BF16),
            pltpu.VMEM((IXP, nz * lanes), F32),
            pltpu.VMEM((planes * IXP, 2 * LP), F32),
            pltpu.VMEM((planes * IXP, 2 * LP), BF16),
            pltpu.VMEM((planes * IXP, 2 * LP), BF16),
            pltpu.VMEM((16, lanes), F32),
            pltpu.VMEM((planes * NG, LP), F32),
            pltpu.VMEM((LP, lanes), F32),
            pltpu.VMEM((slots, NG), F32),
            dma((nz,)), dma((nz,)), dma((3, nz)), dma((3, nz)),
        ]
        + Projector.scratch(nz, slots, rows),
        compiler_params=pltpu.CompilerParams(collective_id=0, has_side_effects=True),
    )(*operands, resident[0].reshape(2 * rows, slots, NG))
    return out[None, None]


def solution(mesh):
    in_specs = (
        P("kpt", "band", None, "plane", None),
        P("kpt", "band", None, "plane", None),
        P("plane", None),
        P("kpt", None),
        P("kpt", None),
    )
    out_specs = P("kpt", "band", None, "plane", None)
    return jax.shard_map(
        functools.partial(on_device, nz=mesh.shape["plane"]),
        mesh=mesh, in_specs=in_specs, out_specs=out_specs, check_vma=False,
    )
```

```python
import functools
import math

import jax
import jax.numpy as jnp
import numpy as np
from jax import lax
from jax.experimental import pallas as pl
from jax.experimental.pallas import tpu as pltpu
from jax.sharding import PartitionSpec as P

NG = 96
KINETIC = 12.0
HIGHEST = lax.Precision.HIGHEST
MESH = pl.DeviceIdType.MESH
RAD = NG // 4
IXP = 64
LP = 128
F32 = jnp.float32
BF16 = jnp.bfloat16


def split_np(table):
    table = np.asarray(table, np.float32)
    high = table.astype(jnp.bfloat16)
    low = (table - high.astype(np.float32)).astype(jnp.bfloat16)
    return high, low


def tables():
    turn = 2.0 * math.pi / NG
    grid = np.arange(NG)
    full = np.outer(grid, grid) % NG * turn
    tz = np.concatenate([np.cos(full), np.sin(full)], axis=0)
    signed = np.arange(IXP) - RAD
    inside = (np.arange(IXP) <= 2 * RAD).astype(np.float64)
    part = np.outer(grid, signed) % NG * turn
    cosine = np.cos(part) * inside
    sine = np.sin(part) * inside
    pad = np.zeros((LP - NG, IXP))
    cy = np.concatenate([cosine, pad])
    sy = np.concatenate([sine, pad])
    ty = np.block([[cy, -sy], [sy, cy]])
    xf = np.block([[cosine, -sine], [sine, cosine]])
    xb = np.block([[cosine.T, sine.T], [-sine.T, cosine.T]]) / float(NG) ** 3
    zb = np.zeros((LP, 2 * LP))
    zb[:NG, :NG] = np.cos(full)
    zb[:NG, LP : LP + NG] = np.sin(full)
    high, low = split_np(xb)
    wide = np.concatenate([high, low, high], axis=1)
    return [np.stack(split_np(table)) for table in (tz, ty, xf)] + [wide, np.stack(split_np(zb))]


def split(value):
    high = value.astype(BF16)
    low = (value - high.astype(F32)).astype(BF16)
    return high, low


def stack3(pair, axis, left):
    high, low = pair
    return jnp.concatenate([high, low, high] if left else [high, high, low], axis)


def contract(left, right, axes):
    dims = (((axes[0],), (axes[1],)), ((), ()))
    return lax.dot_general(left, right, dims, preferred_element_type=F32)


def dot3(left, right, axes):
    if left[0].shape[axes[0]] % LP == 0:
        return contract(stack3(left, axes[0], True), stack3(right, axes[1], False), axes)
    return contract(left[0], right[0], axes) + (
        contract(left[1], right[0], axes) + contract(left[0], right[1], axes)
    )


def local_kernel(
    nz, slots, planes,
    inputs, out_ref,
    wf_ref, table_ref, pot_ref, kp_ref, tz, ty, xf, xb, zb, insem,
    send1, recv1, send2, recv2, bth, btl, lhh, lhl, mask, acc, sph, spl, tabx, weights, trans, livecol,
    ssem1, rsem1, ssem2, rsem2,
    projector,
):
    me = lax.axis_index("plane")
    lanes = send1.shape[2]
    barrier = pltpu.get_barrier_semaphore()
    for step in range(1, nz):
        pl.semaphore_signal(barrier, inc=1, device_id={"plane": lax.rem(me + step, nz)}, device_id_type=MESH)
    greeted = projector.greet(barrier)
    held = (wf_ref, table_ref, pot_ref, kp_ref, tz, ty, xf, xb, zb)
    fetches = [pltpu.make_async_copy(a, b, insem.at[i]) for i, (a, b) in enumerate(zip(inputs, held))]
    for i in (0, 4, 1, 5, 2, 3, 6, 7, 8):
        fetches[i].start()
    fetches[0].wait()
    fetches[4].wait()

    forward = (tz[0], tz[1])
    from_real = dot3(forward, split(wf_ref[0]), (1, 1))
    from_imag = dot3(forward, split(wf_ref[1]), (1, 1))
    real = from_real[:NG] - from_imag[NG:]
    imag = from_imag[:NG] + from_real[NG:]
    send1[:, :, 0:slots] = real.reshape(nz, planes, slots)
    send1[:, :, slots : 2 * slots] = imag.reshape(nz, planes, slots)
    send1[:, :, 2 * slots :] = jnp.zeros((nz, planes, lanes - 2 * slots), F32)
    pl.semaphore_wait(barrier, nz - 1 + greeted)

    def transfer(source, target, ssem, rsem, step):
        there = lax.rem(me + step, nz)
        return pltpu.make_async_remote_copy(
            src_ref=source.at[there],
            dst_ref=target.at[me],
            send_sem=ssem.at[step],
            recv_sem=rsem.at[step],
            device_id={"plane": there},
            device_id_type=MESH,
        )

    out1 = [transfer(send1, recv1, ssem1, rsem1, step) for step in range(1, nz)]
    for step in sorted(range(1, nz), key=lambda i: -min(i, nz - i)):
        out1[step - 1].start()
    projector.start_resident()
    for i in (1, 5, 2, 3, 6, 7, 8):
        fetches[i].wait()

    tabx[...] = jnp.full(tabx.shape, float(NG * NG), F32)
    columns = table_ref[...].astype(F32)
    for q in range(nz):
        part = columns[:, q * slots : (q + 1) * slots]
        tabx[q : q + 1, 0:slots] = part
        tabx[q : q + 1, slots : 2 * slots] = part

    def decode(column):
        ix = ((column + 0.5) * (1.0 / NG)).astype(jnp.int32).astype(F32)
        iy = column - ix * NG
        return jnp.where(ix < NG // 2, ix, ix - NG), jnp.where(iy < NG // 2, iy, iy - NG)

    def block_lanes(q):
        return pl.ds(pl.multiple_of(q * lanes, LP), lanes)

    second = lax.broadcasted_iota(jnp.int32, (1, lanes), 1) >= slots
    rows = lax.broadcasted_iota(jnp.int32, (2 * IXP, lanes), 0).astype(F32)

    @pl.loop(0, nz)
    def _(q):
        column = tabx[pl.ds(q, 1), :]
        alive = column < float(NG * NG)
        mx, my = decode(column)
        kx = jnp.where(alive, mx + RAD, -1.0)
        ky = jnp.where(alive, my + RAD + jnp.where(second, float(IXP), 0.0), -1.0)
        mask[:, block_lanes(q)] = jnp.where(rows[:IXP] == kx, 1.0, 0.0)
        hot = jnp.where(rows == ky, 1.0, 0.0).astype(BF16)
        for i, into in ((0, bth), (1, btl)):
            into[:, block_lanes(q)] = jnp.dot(ty[i], hot, preferred_element_type=F32).astype(BF16)

    zeros = jnp.zeros((weights.shape[0], LP - NG), F32)
    weights[:, NG:LP] = zeros
    for x in range(NG):
        weights[pl.ds(x, planes, stride=NG), 0:NG] = pot_ref[:, x * NG : (x + 1) * NG]

    recv1[me] = send1[me]
    acc[...] = jnp.zeros(acc.shape, F32)
    deep = planes * IXP // 2

    def pair_of(pair):
        return lax.rem(me + nz - pair, nz), lax.rem(me + pair + 1, nz)

    @pl.loop(0, nz // 2)
    def _(pair):
        owners = pair_of(pair)

        @pl.when(pair > 0)
        def _():
            transfer(send1, recv1, ssem1, rsem1, pair).wait_recv()

        transfer(send1, recv1, ssem1, rsem1, nz - 1 - pair).wait_recv()
        for place, q in enumerate(owners):
            values = recv1[q]
            hot = mask[:, block_lanes(q)].astype(BF16)
            into = slice(place * lanes, (place + 1) * lanes)
            for z in range(planes):
                high, low = split(jnp.broadcast_to(values[z : z + 1], (16, lanes)))
                for g in range(IXP // 16):
                    part = hot[g * 16 : (g + 1) * 16]
                    at = slice(z * IXP + g * 16, z * IXP + (g + 1) * 16)
                    lhh[0, at, into] = part * high
                    lhl[0, at, into] = part * low
        phase = tuple(jnp.concatenate([b[:, block_lanes(q)] for q in owners], 1) for b in (bth, btl))
        for h in range(2):
            at = slice(h * deep, (h + 1) * deep)
            acc[at] = acc[at] + dot3((lhh[0, at], lhl[0, at]), phase, (1, 1))

    to_x = (xf[0], xf[1])
    to_k = xb[...]

    @pl.loop(0, planes // 4)
    def _(quad):
        for z2 in range(0, 4, 2):
            z = quad * 4 + z2
            a = acc[pl.ds(pl.multiple_of(z * IXP, IXP), IXP)]
            b = acc[pl.ds(pl.multiple_of((z + 1) * IXP, IXP), IXP)]
            joined = jnp.concatenate(
                [jnp.concatenate([a[:, :LP], b[:, :LP]], 1), jnp.concatenate([a[:, LP:], b[:, LP:]], 1)], 0
            )
            field = dot3(to_x, split(joined), (1, 0))
            weight = jnp.concatenate(
                [weights[pl.ds(pl.multiple_of((z + h) * NG, 8), NG)] for h in range(2)], 1
            )
            product = field * jnp.concatenate([weight, weight], 0)
            back = contract(to_k, stack3(split(product), 0, False), (1, 0))
            for h in range(2):
                high, low = split(
                    jnp.concatenate([back[:IXP, h * LP : (h + 1) * LP], back[IXP:, h * LP : (h + 1) * LP]], 1)
                )
                at = pl.ds(pl.multiple_of((z + h) * IXP, IXP), IXP)
                sph[at], spl[at] = high, low

    @pl.loop(0, nz // 2)
    def _(turn):
        pair = nz // 2 - 1 - turn
        owners = pair_of(pair)
        phase = tuple(jnp.concatenate([b[:, block_lanes(q)] for q in owners], 1) for b in (bth, btl))
        hot = jnp.concatenate([mask[:, block_lanes(q)] for q in owners], 1)
        halves = []
        for h in range(2):
            at = slice(h * deep, (h + 1) * deep)
            found = dot3((sph[at], spl[at]), phase, (1, 0))
            halves.append(jnp.sum(found.reshape(planes // 2, IXP, 2 * lanes) * hot[None], axis=1))
        picked = jnp.concatenate(halves, 0)
        for place, q in enumerate(owners):
            send2[q] = picked[:, place * lanes : (place + 1) * lanes]

        @pl.when(pair > 0)
        def _():
            transfer(send2, recv2, ssem2, rsem2, nz - pair).start()

        transfer(send2, recv2, ssem2, rsem2, pair + 1).start()

    recv2[me] = send2[me]
    out2 = [transfer(send2, recv2, ssem2, rsem2, step) for step in range(1, nz)]

    column = tabx[pl.ds(me, 1), :]
    mx, my = decode(column)
    fx = mx + kp_ref[0:1, 0:1]
    fy = my + kp_ref[0:1, 1:2]
    trans[NG:, :] = jnp.zeros((LP - NG, lanes), F32)
    trans[NG : NG + 1, :] = fx * fx + fy * fy
    trans[NG + 1 : NG + 2, :] = jnp.where(column < float(NG * NG), 1.0, 0.0)
    freq = lax.broadcasted_iota(jnp.int32, (1, NG), 1)
    fz = jnp.where(freq < NG // 2, freq, freq - NG).astype(F32) + kp_ref[0:1, 2:3]
    projector.finish_resident()
    projector.flatten_resident()
    for copy in out1:
        copy.wait_send()
    for copy in out2:
        copy.wait()
    trans[0:NG, :] = recv2[...].reshape(NG, lanes)
    turned = trans[...].T
    result = dot3(split(turned[: 2 * slots]), (zb[0], zb[1]), (1, 0))
    alive = turned[:slots, NG + 1 : NG + 2]
    kinetic = (KINETIC / (NG * NG)) * (turned[:slots, NG : NG + 1] + fz * fz) * alive
    images = (
        (result[:slots, :LP] + result[slots:, LP:])[:, :NG] + kinetic * wf_ref[0],
        (result[slots:, :LP] - result[:slots, LP:])[:, :NG] + kinetic * wf_ref[1],
    )
    projector.pack(images)
    for c in range(2):
        out_ref[c] = images[c]
    livecol[...] = jnp.broadcast_to(alive, livecol.shape)
    first_gram = projector.gather()
    projector.correct(projector.margin(first_gram))
    projector.scatter()
    for c in range(2):
        out_ref[c] = out_ref[c] - livecol[...] * projector.correction(c)


ORDER = (0, 1, 7, 2, 6, 3, 5, 4)


class Projector:
    def __init__(self, nz, slots, rows, refs):
        (self.res, self.dbuf, self.dh, self.dl, self.packed, self.abuf, self.ih, self.il, self.mpair, self.mall,
         self.cbuf, self.rbuf, self.fbuf, self.unpacked,
         self.dsem, self.psem, self.agsem, self.mpsem, self.mssem, self.mrsem, self.rssem, self.fsem) = refs
        self.nz, self.half, self.rows = nz, slots // 2, rows
        self.lines = self.half * NG // LP
        self.block = 2 * self.lines
        self.parts = ((0, 64), (64, self.block - 64))
        band = lax.axis_index("band")
        nb = 16
        self.me = lax.axis_index("plane")
        self.core = lax.rem(band, 2)
        self.partner = {"band": band + 1 - 2 * self.core}
        chip = band - self.core
        self.sides = (lax.rem(chip + 2, nb), lax.rem(chip + nb - 2, nb))

    def beside(self, way, core):
        return {"band": self.sides[way] + core}

    def remote(self, src, dst, send, recv, device):
        return pltpu.make_async_remote_copy(
            src_ref=src, dst_ref=dst, send_sem=send, recv_sem=recv, device_id=device, device_id_type=MESH
        )

    def greet(self, barrier):
        others = [self.beside(way, core) for way in range(2) for core in range(2)]
        for device in [self.partner] + others:
            pl.semaphore_signal(barrier, inc=1, device_id=device, device_id_type=MESH)
        return 5

    def slab(self, i):
        place = (self.core * self.rows * 2 + i) * self.half
        return self.dbuf.at[pl.ds(pl.multiple_of(place, 8), self.half), :]

    def local_fetch(self, i):
        own = pl.ds(pl.multiple_of(self.core * self.half, 8), self.half)
        return pltpu.make_async_copy(self.res.at[i, own, :], self.slab(i), self.dsem.at[0, i])

    def swap_resident(self, i):
        other = pl.ds(pl.multiple_of((1 - self.core) * self.half, 8), self.half)
        return self.remote(
            self.res.at[i, other, :], self.slab(i), self.dsem.at[1, i], self.dsem.at[2, i], self.partner
        )

    def start_resident(self):
        @pl.loop(0, 2 * self.rows)
        def _(i):
            self.swap_resident(i).start()
            self.local_fetch(i).start()

    def finish_resident(self):
        @pl.loop(0, 2 * self.rows)
        def _(i):
            self.swap_resident(i).wait()
            self.local_fetch(i).wait()

    def flatten_resident(self):
        third = self.lines // 3
        span = 2 * self.half

        @pl.loop(0, third)
        def _(i):
            for c in range(2):
                for group in range(2 * self.rows // 16):
                    base = group * 16 * span + c * self.half + i
                    tail = self.dbuf[pl.ds(base + self.lines, 16, stride=span), :]
                    for k in range(3):
                        head = self.dbuf[pl.ds(base + k * third, 16, stride=span), :]
                        line = jnp.concatenate([head, tail[:, k * 32 : (k + 1) * 32]], 1)
                        lanes = pl.ds(pl.multiple_of((k * third + i) * LP, LP), LP)
                        at = slice(c * 2 * self.rows + group * 16, c * 2 * self.rows + group * 16 + 16)
                        self.dh[at, lanes], self.dl[at, lanes] = split(line)

    def at(self, rel, sub, part=None):
        place = (ORDER.index(rel % 8) * 2 + sub) * self.block
        if part is None:
            return pl.ds(pl.multiple_of(place, 8), self.block)
        start, size = self.parts[part]
        return pl.ds(pl.multiple_of(place + start, 8), size)

    def pack(self, images):
        third = self.lines // 3
        for hh in range(2):
            for c in range(2):
                part = images[c][hh * self.half : (hh + 1) * self.half]
                self.packed[hh, c * self.lines : (c + 1) * self.lines, 0:NG] = part[: self.lines, :NG]
                for k in range(3):
                    start = c * self.lines + k * third
                    self.packed[hh, start : start + third, NG:LP] = part[self.lines :, k * 32 : (k + 1) * 32]

    def gather(self):
        mine, other = self.core, 1 - self.core
        pair = self.remote(
            self.packed.at[other], self.abuf.at[self.at(0, mine)], self.psem.at[0], self.psem.at[1], self.partner
        )
        sign = (-1, 1)

        def first(way, core, part):
            start, size = self.parts[part]
            return self.remote(
                self.packed.at[core, pl.ds(start, size)], self.abuf.at[self.at(sign[way], mine, part)],
                self.agsem.at[0, way, 0, core, part], self.agsem.at[1, way, 0, mine, part], self.beside(way, core),
            )

        def hop(way, step, sub, part):
            return self.remote(
                self.abuf.at[self.at(sign[way] * step, sub, part)],
                self.abuf.at[self.at(sign[way] * (step + 1), sub, part)],
                self.agsem.at[0, way, step, sub, part], self.agsem.at[1, way, step, sub, part],
                self.beside(way, mine),
            )

        started = [first(way, core, part) for part in range(2) for core in range(2) for way in range(2)]
        for copy in started:
            copy.start()
        pair.start()
        self.abuf[self.at(0, mine), :] = self.packed[mine]
        for step in (1, 2, 3):
            if step == 3:
                pair.wait()
                self.flatten_images(0)
            for part in range(2):
                for sub in range(2):
                    for way in range(2):
                        if step == 3 and sub != way:
                            continue
                        hop(way, step - 1, sub, part).wait_recv()
                        copy = hop(way, step, sub, part)
                        copy.start()
                        started.append(copy)
        first_gram = self.gram(0)
        for part in range(2):
            for way in range(2):
                hop(way, 2, 1 - way, part).wait_recv()
                hop(way, 3, way, part).wait_recv()
        for copy in started:
            copy.wait_send()
        return first_gram

    def flatten_images(self, group):
        @pl.loop(0, self.lines)
        def _(r):
            lanes = pl.ds(pl.multiple_of(r * LP, LP), LP)
            value = jnp.concatenate(
                [
                    self.abuf[pl.ds(group * 8 * self.block + c * self.lines + r, 8, stride=self.block), :]
                    for c in range(2)
                ],
                0,
            )
            self.ih[group, :, lanes], self.il[group, :, lanes] = split(value)

    def gram(self, group):
        count = 2 * self.rows
        middle = self.lines // 2 * LP
        gram = sum(
            dot3((self.ih[group, :, k], self.il[group, :, k]), (self.dh[:, k], self.dl[:, k]), (1, 1))
            for k in (slice(0, middle), slice(middle, 2 * middle))
        )
        real = gram[:8, :count] + gram[8:, count:]
        imag = gram[8:, :count] - gram[:8, count:]
        return jnp.concatenate([real, imag], 1)

    def margin(self, first_gram):
        self.flatten_images(1)
        count = 2 * self.rows
        self.mpair[0] = jnp.concatenate([first_gram, self.gram(1)], 1)
        swap = self.remote(self.mpair.at[0], self.mpair.at[1], self.mpsem.at[0], self.mpsem.at[1], self.partner)
        swap.start()
        swap.wait()
        self.mall[self.me] = self.mpair[0] + self.mpair[1]
        copies = []
        for step in sorted(range(1, self.nz), key=lambda i: -min(i, self.nz - i)):
            copy = self.remote(
                self.mall.at[self.me], self.mall.at[self.me],
                self.mssem.at[step], self.mrsem.at[step], {"plane": lax.rem(self.me + step, self.nz)},
            )
            copy.start()
            copies.append(copy)
        for copy in copies:
            copy.wait()
        flat = jnp.sum(self.mall[...], axis=0)
        both = jnp.concatenate([flat[:, : 2 * count], flat[:, 2 * count :]], 0)
        real, imag = both[:, :count], both[:, count:]
        return jnp.concatenate(
            [jnp.concatenate([real, -imag], 1), jnp.concatenate([imag, real], 1)], 0
        )

    def correct(self, margin):
        left = stack3(split(margin), 1, True)
        batch = 4

        @pl.loop(0, self.lines // batch)
        def _(g):
            lanes = pl.ds(pl.multiple_of(g * batch * LP, LP), batch * LP)
            right = stack3((self.dh[:, lanes], self.dl[:, lanes]), 0, False)
            middle = batch // 2 * LP
            value = jnp.concatenate(
                [contract(left, right[:, :middle], (1, 0)), contract(left, right[:, middle:], (1, 0))], 1
            )
            for i in range(batch):
                for c in range(2):
                    self.cbuf[pl.ds(c * self.lines + g * batch + i, 16, stride=self.block), :] = value[
                        c * 16 : (c + 1) * 16, i * LP : (i + 1) * LP
                    ]

    def scatter(self):
        mine, other = self.core, 1 - self.core

        def slot(way, k, sub, part=None):
            place = ((way * 4 + k) * 2 + sub) * self.block
            start, size = (0, self.block) if part is None else self.parts[part]
            return pl.ds(pl.multiple_of(place + start, 8), size)

        def own(way, k, sub, part):
            return self.at(k if way == 0 else -k, sub, part)

        def hop(way, k, sub, part, source):
            if k == 1:
                target, device = mine, self.beside(way, sub)
            else:
                target, device = sub, self.beside(way, mine)
            return self.remote(
                source, self.rbuf.at[slot(way, k - 1, target, part)],
                self.rssem.at[0, way, k - 1, sub, part], self.rssem.at[1, way, k - 1, target, part], device,
            )

        def arrived(way, k, index, part):
            here = self.rbuf.at[slot(way, k, index, part)]
            return self.remote(
                here, here, self.rssem.at[0, way, k, index, part], self.rssem.at[1, way, k, index, part],
                self.beside(way, mine),
            )

        sent = []
        for k in (4, 3, 2, 1):
            for part in range(2):
                for sub in range(2):
                    for way in range(2):
                        first = 4 if sub == way else 3
                        if k > first:
                            continue
                        source = self.cbuf.at[own(way, k, sub, part)]
                        if k < first:
                            arrived(way, k, sub, part).wait_recv()
                            here = slot(way, k, sub, part)
                            self.rbuf[here, :] = self.rbuf[here, :] + self.cbuf[own(way, k, sub, part), :]
                            source = self.rbuf.at[here]
                        copy = hop(way, k, sub, part, source)
                        copy.start()
                        sent.append(copy)
            if k == 3:
                copy = self.remote(
                    self.cbuf.at[self.at(0, other)], self.fbuf.at[2], self.fsem.at[0], self.fsem.at[1], self.partner
                )
                copy.start()
        for part in range(2):
            for index in range(2):
                for way in range(2):
                    arrived(way, 0, index, part).wait_recv()
        arrivals = [self.rbuf[slot(0, 0, half), :] + self.rbuf[slot(1, 0, half), :] for half in (mine, other)]
        self.fbuf[0] = self.cbuf[self.at(0, mine), :] + arrivals[0]
        self.finish_pair(other)
        self.fbuf[1] = self.fbuf[2] + arrivals[1]
        for copy in sent:
            copy.wait_send()
        self.unpack(0, mine)
        self.unpack(1, other)

    def finish_pair(self, other):
        self.remote(
            self.cbuf.at[self.at(0, other)], self.fbuf.at[2], self.fsem.at[0], self.fsem.at[1], self.partner
        ).wait()

    def unpack(self, source, hh):
        third = self.lines // 3
        for c in range(2):
            start = c * self.lines
            self.unpacked[hh, c, 0 : self.lines, :] = self.fbuf[source, start : start + self.lines, 0:NG]
            for k in range(3):
                self.unpacked[hh, c, self.lines : self.half, k * 32 : (k + 1) * 32] = self.fbuf[
                    source, start + k * third : start + (k + 1) * third, NG:LP
                ]

    def correction(self, c):
        return jnp.concatenate([self.unpacked[0, c], self.unpacked[1, c]], 0)

    @staticmethod
    def scratch(nz, slots, rows):
        half = slots // 2
        lines = half * NG // LP
        block = 2 * lines
        dma = pltpu.SemaphoreType.DMA
        return [
            pltpu.VMEM((4 * rows * half, NG), F32),
            pltpu.VMEM((4 * rows, lines * LP), BF16),
            pltpu.VMEM((4 * rows, lines * LP), BF16),
            pltpu.VMEM((2, block, LP), F32),
            pltpu.VMEM((16 * block, LP), F32),
            pltpu.VMEM((2, 16, lines * LP), BF16),
            pltpu.VMEM((2, 16, lines * LP), BF16),
            pltpu.VMEM((2, 8, LP), F32),
            pltpu.VMEM((nz, 8, LP), F32),
            pltpu.VMEM((16 * block, LP), F32),
            pltpu.VMEM((16 * block, LP), F32),
            pltpu.VMEM((3, block, LP), F32),
            pltpu.VMEM((2, 2, half, NG), F32),
            dma((3, 2 * rows)), dma((2,)), dma((2, 2, 4, 2, 2)), dma((2,)), dma((nz,)), dma((nz,)), dma((2, 2, 4, 2, 2)), dma((2,)),
        ]


def kernel(nz, slots, planes, rows, *refs):
    inputs, resident, out_ref, rest = refs[:9], refs[9], refs[10], refs[11:]
    count = 30
    projector = Projector(nz, slots, rows, (resident,) + rest[count:])
    local_kernel(nz, slots, planes, inputs, out_ref, *rest[:count], projector=projector)


def on_device(wavefunctions, resident, potential, stick_column_table, kpoint, nz):
    slots = wavefunctions.shape[3]
    planes = potential.shape[0]
    rows = resident.shape[1]
    lanes = -(-2 * slots // LP) * LP
    consts = [jnp.asarray(t) for t in tables()]
    block = pltpu.VMEM((nz, planes, lanes), F32)
    dma = pltpu.SemaphoreType.DMA
    operands = (wavefunctions[0, 0], stick_column_table, potential, kpoint, *consts)
    out = pl.pallas_call(
        functools.partial(kernel, nz, slots, planes, rows),
        out_shape=jax.ShapeDtypeStruct((2, slots, NG), F32),
        in_specs=[pl.BlockSpec(memory_space=pl.ANY)] * 10,
        out_specs=pl.BlockSpec(memory_space=pltpu.VMEM),
        scratch_shapes=[pltpu.VMEM(x.shape, x.dtype) for x in operands]
        + [
            dma((9,)),
            block, block, block, block,
            pltpu.VMEM((2 * LP, nz * lanes), BF16),
            pltpu.VMEM((2 * LP, nz * lanes), BF16),
            pltpu.VMEM((2, planes * IXP, 2 * lanes), BF16),
            pltpu.VMEM((2, planes * IXP, 2 * lanes), BF16),
            pltpu.VMEM((IXP, nz * lanes), F32),
            pltpu.VMEM((planes * IXP, 2 * LP), F32),
            pltpu.VMEM((planes * IXP, 2 * LP), BF16),
            pltpu.VMEM((planes * IXP, 2 * LP), BF16),
            pltpu.VMEM((16, lanes), F32),
            pltpu.VMEM((planes * NG, LP), F32),
            pltpu.VMEM((LP, lanes), F32),
            pltpu.VMEM((slots, NG), F32),
            dma((nz,)), dma((nz,)), dma((nz,)), dma((nz,)),
        ]
        + Projector.scratch(nz, slots, rows),
        compiler_params=pltpu.CompilerParams(collective_id=0, has_side_effects=True),
    )(*operands, resident[0].reshape(2 * rows, slots, NG))
    return out[None, None]


def solution(mesh):
    in_specs = (
        P("kpt", "band", None, "plane", None),
        P("kpt", "band", None, "plane", None),
        P("plane", None),
        P("kpt", None),
        P("kpt", None),
    )
    out_specs = P("kpt", "band", None, "plane", None)
    return jax.shard_map(
        functools.partial(on_device, nz=mesh.shape["plane"]),
        mesh=mesh, in_specs=in_specs, out_specs=out_specs, check_vma=False,
    )
```
